128 devices in a mesh: sec: 4 (over y), bulk: 32 (over x, z, core).
Axes of the slice: x: 4, y: 4, z: 4, core: 2. Of those that a mesh axis runs over, the one named last changes fastest.
Arguments:
- displacement: float32 [3, 16384], P(None, ('sec', 'bulk')), may hold values from -6 to 6
- nodal_load: float32 [3, 16384], P(None, ('sec', 'bulk')), may hold values from -12 to 12
- connectivity: int32 [4, 65536], P(None, ('sec', 'bulk')), may hold values from 0 to 127
- shape_grads: float32 [12, 65536], P(None, ('sec', 'bulk'))
- elem_volume: float32 [65536], P(('sec', 'bulk')), may hold values from 0.3 to 3
- point_map: int32 [65536], P(('sec', 'bulk')), may hold values from 0 to 65535, as said below
- vol_blocks: int32 [32, 8], P('bulk'), may hold values from 1 to 4, as said below
- c_affine: float32 [32, 8, 36], P('bulk')
- coupling: float32 [20, 32, 6, 128], P(None, 'bulk'), may hold values from -15 to 15
- diag_blocks: bfloat16 [20, 32, 128, 128], P(None, 'bulk'), as said below
- diag_normal: float32 [20, 32, 6], P(None, 'bulk'), may hold values from -4 to 4
- off_blocks: bfloat16 [32, 32, 128, 128], P(None, 'bulk'), may hold values from -0.5 to 0.5
- off_row: int32 [32, 32], P(None, 'bulk'), may hold values from 0 to 19, as said below
- off_col: int32 [32, 32], P(None, 'bulk'), may hold values from 0 to 19, as said below
- off_normal: float32 [32, 32, 6], P(None, 'bulk'), may hold values from -4 to 4
- off_count: int32 [32], P('bulk'), may hold values from 4 to 32, as said below
- fluct_state: bfloat16 [65536, 3072], P(('sec', 'bulk')), as said below
Outputs:
- residual: float32 [3, 16384], P(None, ('sec', 'bulk'))
- product: float32 [3, 16384], P(None, ('sec', 'bulk'))
- update: float32 [3, 16384], P(None, ('sec', 'bulk'))
- fluct_new: bfloat16 [65536, 3072], P(('sec', 'bulk'))
The draws below stay inside these ranges and needn't reach their ends.
Inputs may be any that keep to these rules, and one draw needn't show every extreme that they name: o = point_map[e] // 512 is the serving device, in the order of sec and bulk with sec slowest, and p = point_map[e] % 512 its slot; values are distinct. Device s sends exactly 4 points to every server, 1 of them in volumes with c block rows for each c = 1 .. 4: among the server's slots whose volume has c block rows, taken in increasing order, the one numbered s. `vol_blocks`: each group has 2 volumes of each size from 1 to 4, so 20 block rows in all. `off_row`: A contact's row and column lie in the block rows of one volume of its group, and differ unless that volume has one block row. `off_col`: see off_row. Slots below off_count of a group are in use, the others are not; a multiple of 4, and one group uses all slots. `diag_blocks`: the diagonal entries of every diagonal block lie between 2.5 and 6.5. `fluct_state`: levels a >= the block rows of the point's volume are zero.
All inputs are finite; a program needn't handle non-finite values.
Results may differ from the reference program's by a relative error of at most 0.001.
The reference program's roundings to bfloat16 on the way count: a program that leaves them out, or rounds other values in their place, can miss the bound.
Values may be sent and summed in bfloat16 or wider, within the bound.
A program may use at most 128 MiB of HBM per device.

```python
import math
import jax
import jax.numpy as jnp
from jax import lax

BS = 128
NBMAX = 4
VOL_GRP = 8
GPV_DEV = 64
SWEEPS = 3
ELEM_DEV = 512
NODE_DEV = 128
ELEMS = 65536
NODES = 16384
CAP = 4
ROWS_GRP = 20
OFF_GRP = 32
N_SEC = 4
N_BULK = 32


def volume_sizes(key):
    key_list = jax.random.split(jax.random.fold_in(key, 101), N_BULK)
    size_cycle = (jnp.arange(VOL_GRP, dtype=jnp.int32) % NBMAX + 1).astype(jnp.int32)
    return jax.vmap(lambda subkey: jax.random.permutation(subkey, size_cycle))(key_list).astype(jnp.int32)


def contact_pattern(key):
    vol_sizes = volume_sizes(key)
    starts = (jnp.cumsum(vol_sizes, axis=1) - vol_sizes).astype(jnp.int32)
    key_list = jax.random.split(jax.random.fold_in(key, 202), 5)
    vol_pick = jax.random.randint(key_list[0], (N_BULK, OFF_GRP), 0, VOL_GRP)
    row_counts = jnp.take_along_axis(vol_sizes, vol_pick, axis=1)
    row_starts = jnp.take_along_axis(starts, vol_pick, axis=1)
    level_one = jax.random.randint(key_list[1], (N_BULK, OFF_GRP), 0, row_counts)
    offset_pick = jax.random.randint(key_list[2], (N_BULK, OFF_GRP), 0, jnp.maximum(row_counts - 1, 1))
    level_two = (level_one + 1 + offset_pick) % row_counts
    load_level = jax.random.randint(key_list[3], (N_BULK,), 1, 5)
    heavy_group = jax.random.randint(key_list[4], (), 0, N_BULK)
    group_ids = jnp.arange(N_BULK, dtype=jnp.int32)
    load_level = jnp.where(group_ids == heavy_group, 8, load_level)
    load_level = jnp.where(group_ids == (heavy_group + 1) % N_BULK, 1, load_level)
    row_pick = (row_starts + level_one).astype(jnp.int32).T
    col_pick = (row_starts + level_two).astype(jnp.int32).T
    return (row_pick, col_pick, (load_level * (OFF_GRP // 8)).astype(jnp.int32))


def draw_point_map(key, part):
    devices = N_SEC * N_BULK
    per_class = CAP // NBMAX
    vol_sizes = volume_sizes(key)
    vol_ids = jnp.arange(VOL_GRP, dtype=jnp.int32)
    earlier = (vol_sizes[:, None, :] == vol_sizes[:, :, None]) & (vol_ids[None, None, :] < vol_ids[None, :, None])
    vol_rank = jnp.sum(earlier.astype(jnp.int32), axis=2).astype(jnp.int32)
    slot_ids = jnp.arange(ELEM_DEV, dtype=jnp.int32)
    slot_rank = vol_rank[:, slot_ids // GPV_DEV] * GPV_DEV + slot_ids[None, :] % GPV_DEV
    slot_class = vol_sizes[:, slot_ids // GPV_DEV]
    slot_code = (slot_rank // per_class * NBMAX + slot_class - 1) * per_class + slot_rank % per_class
    group_rows = jnp.broadcast_to(jnp.arange(N_BULK, dtype=jnp.int32)[:, None], (N_BULK, ELEM_DEV))
    slot_table = jnp.zeros((N_BULK, ELEM_DEV), jnp.int32).at[group_rows, slot_code].set(jnp.broadcast_to(slot_ids[None, :], (N_BULK, ELEM_DEV)))
    key_list = jax.random.split(jax.random.fold_in(key, 303), devices)
    shuffles = jax.vmap(lambda subkey: jax.random.permutation(subkey, ELEM_DEV))(key_list).astype(jnp.int32)
    source = jnp.arange(devices, dtype=jnp.int32)[:, None]
    owner_id = shuffles // CAP
    position = shuffles % CAP
    chosen_slot = slot_table[owner_id % N_BULK, source * CAP + position]
    return (owner_id * ELEM_DEV + chosen_slot).reshape(-1).astype(jnp.int32)


def draw_vol_blocks(key, part):
    return volume_sizes(key)


def draw_off_row(key, part):
    return contact_pattern(key)[0]


def draw_off_col(key, part):
    return contact_pattern(key)[1]


def draw_off_count(key, part):
    return contact_pattern(key)[2]


def draw_shape_grads(key, part):
    devices = N_SEC * N_BULK
    position = (jnp.arange(ELEMS, dtype=jnp.int32) // ELEM_DEV).astype(jnp.float32) / max(devices - 1, 1)
    subkey = jax.random.fold_in(key, 505)
    entries = 0.3 * jax.random.normal(subkey, (12, ELEMS), jnp.float32)
    growth = 3.0 ** (0.25 * position)
    return entries * growth[None, :]


def draw_c_affine(key, part):
    key_list = jax.random.split(jax.random.fold_in(key, 606), 2)
    gaussian = jax.random.normal(key_list[0], (N_BULK, VOL_GRP, 6, 6), jnp.float32)
    symmetric = 0.25 * (gaussian + jnp.swapaxes(gaussian, 2, 3))
    diag_vals = jax.random.uniform(key_list[1], (N_BULK, VOL_GRP, 6), jnp.float32, 4.0, 6.0)
    identity = jnp.eye(6, dtype=jnp.float32)
    full = symmetric * (1.0 - identity) + identity * diag_vals[:, :, :, None]
    return full.reshape(N_BULK, VOL_GRP, 36)


def draw_diag_blocks(key, part):
    key_list = jax.random.split(jax.random.fold_in(key, 707), 2)
    full_shape = (ROWS_GRP, N_BULK, BS, BS)
    identity = jnp.eye(BS, dtype=bool)
    off_entries = 0.22 * jax.random.normal(key_list[0], full_shape, jnp.float32)
    diag_entries = jax.random.uniform(key_list[1], full_shape, jnp.float32, 3.0, 6.0)
    return jnp.where(identity, diag_entries, off_entries).astype(jnp.bfloat16)


def draw_fluct_state(key, part):
    slot_codes = draw_point_map(key, part)
    vol_sizes = volume_sizes(key)
    owner_id = slot_codes // ELEM_DEV
    within = slot_codes % ELEM_DEV
    row_counts = vol_sizes[owner_id % N_BULK, within // GPV_DEV]
    live_rows = (jnp.arange(NBMAX, dtype=jnp.int32)[None, :] < row_counts[:, None]).astype(jnp.float32)
    subkey = jax.random.fold_in(key, 404)
    entries = 0.5 * jax.random.normal(subkey, (ELEMS, NBMAX, BS * 6), jnp.float32)
    return (entries * live_rows[:, :, None]).reshape(ELEMS, NBMAX * BS * 6).astype(jnp.bfloat16)


def set_ends(values, rng, smallest, largest):
    place = [jax.random.randint(jax.random.fold_in(rng, axis), (), 0, length) for axis, length in enumerate(values.shape)]
    widest = values.shape.index(max(values.shape))
    next_to = place[:widest] + [(place[widest] + 1) % values.shape[widest]] + place[widest + 1:]
    return values.at[tuple(place)].set(smallest).at[tuple(next_to)].set(largest)


def block_levels(rng, shape, shards, low, largest):
    def one(dim, parts):
        steps = jax.random.uniform(jax.random.fold_in(jax.random.fold_in(rng, 6), dim), (parts,), jnp.float32, low / len(shards), largest / len(shards))
        return jnp.repeat(jnp.exp(steps), shape[dim] // parts).reshape((-1,) + (1,) * (len(shape) - dim - 1))

    loudness = one(*shards[0])
    for cut in shards[1:]:
        loudness = loudness * one(*cut)
    return loudness


def normal_values(stream_key, shape, scale, reach, cuts=(), held_as=jnp.bfloat16):
    drawn = scale * jax.random.normal(stream_key, shape, jnp.float32)
    if cuts:
        drawn = drawn * block_levels(stream_key, shape, cuts, -0.22, 0.18)
    return jnp.clip(drawn, -reach, reach).astype(held_as)


def setup_inputs(seed: int = 0) -> dict:
    key_of = jax.random.split(jax.random.key(seed), 18)
    displacement = normal_values(key_of[0], (3, NODES), 1.0, 6.0, ((1, 128),), jnp.float32)
    nodal_load = normal_values(key_of[1], (3, NODES), 2.0, 12.0, ((1, 128),), jnp.float32)
    connectivity = set_ends(jax.random.randint(key_of[2], (4, ELEMS), 0, NODE_DEV), jax.random.fold_in(key_of[2], 1), 0, NODE_DEV - 1).astype(jnp.int32)
    shape_grads = draw_shape_grads(jax.random.fold_in(key_of[17], 71), 0)
    elem_volume = jnp.clip(jnp.exp(math.log(3.0) - 2.3025851 * jax.random.uniform(key_of[4], (ELEMS,), jnp.float32) ** block_levels(key_of[4], (ELEMS,), ((0, 128),), -0.2, 0.2)), 0.3, 3.0)
    point_map = draw_point_map(jax.random.fold_in(key_of[17], 71), 0)
    vol_blocks = draw_vol_blocks(jax.random.fold_in(key_of[17], 71), 0)
    c_affine = draw_c_affine(jax.random.fold_in(key_of[17], 71), 0)
    coupling = normal_values(key_of[8], (ROWS_GRP, N_BULK, 6, BS), 2.5, 15.0, ((1, 32),), jnp.float32)
    diag_blocks = draw_diag_blocks(jax.random.fold_in(key_of[17], 71), 0)
    diag_normal = normal_values(key_of[10], (ROWS_GRP, N_BULK, 6), 0.7, 4.0, ((1, 32),), jnp.float32)
    off_blocks = normal_values(key_of[11], (OFF_GRP, N_BULK, BS, BS), 0.08, 0.5, ((1, 32),))
    off_row = draw_off_row(jax.random.fold_in(key_of[17], 71), 0)
    off_col = draw_off_col(jax.random.fold_in(key_of[17], 71), 0)
    off_normal = normal_values(key_of[14], (OFF_GRP, N_BULK, 6), 0.7, 4.0, ((1, 32),), jnp.float32)
    off_count = draw_off_count(jax.random.fold_in(key_of[17], 71), 0)
    fluct_state = draw_fluct_state(jax.random.fold_in(key_of[17], 71), 0)
    return {"displacement": displacement, "nodal_load": nodal_load, "connectivity": connectivity, "shape_grads": shape_grads, "elem_volume": elem_volume, "point_map": point_map, "vol_blocks": vol_blocks, "c_affine": c_affine, "coupling": coupling, "diag_blocks": diag_blocks, "diag_normal": diag_normal, "off_blocks": off_blocks, "off_row": off_row, "off_col": off_col, "off_normal": off_normal, "off_count": off_count, "fluct_state": fluct_state}


HIGHEST_PREC = lax.Precision.HIGHEST
GAIN_NORMAL = 0.4
CLIP_RMS = 1.0

def strain_of(shape_grads, nodal):
    shaped = shape_grads.reshape(4, 3, -1)
    grad_x, grad_y, grad_z = (shaped[:, 0], shaped[:, 1], shaped[:, 2])
    disp_x, disp_y, disp_z = (nodal[0], nodal[1], nodal[2])
    return jnp.stack([lax.optimization_barrier(jnp.sum(grad_x * disp_x, axis=0)), lax.optimization_barrier(jnp.sum(grad_y * disp_y, axis=0)), lax.optimization_barrier(jnp.sum(grad_z * disp_z, axis=0)), lax.optimization_barrier(jnp.sum(grad_z * disp_y + grad_y * disp_z, axis=0)), lax.optimization_barrier(jnp.sum(grad_z * disp_x + grad_x * disp_z, axis=0)), lax.optimization_barrier(jnp.sum(grad_y * disp_x + grad_x * disp_y, axis=0))])

def forces_of(shape_grads, stress):
    shaped = shape_grads.reshape(4, 3, -1)
    grad_x, grad_y, grad_z = (shaped[:, 0], shaped[:, 1], shaped[:, 2])
    force_x = grad_x * stress[0] + grad_z * stress[4] + grad_y * stress[5]
    force_y = grad_y * stress[1] + grad_z * stress[3] + grad_x * stress[5]
    force_z = grad_z * stress[2] + grad_y * stress[3] + grad_x * stress[4]
    return jnp.stack([force_x, force_y, force_z])

def apply_tangent(tangent_cols, strain):
    return lax.optimization_barrier(jnp.sum(tangent_cols.reshape(6, 6, -1) * strain[None, :, :], axis=1))

def assemble(forces, node_ids, node_total):
    flat_ids = node_ids.reshape(-1)
    return jnp.stack([jax.ops.segment_sum(forces[component].reshape(-1), flat_ids, num_segments=node_total) for component in range(3)])

def row_layout(vol_sizes):
    row_ends = jnp.cumsum(vol_sizes).astype(jnp.int32)
    starts = (row_ends - vol_sizes).astype(jnp.int32)
    row_ids = jnp.arange(ROWS_GRP, dtype=jnp.int32)
    row_volume = lax.optimization_barrier(jnp.sum((row_ids[:, None] >= row_ends[None, :]).astype(jnp.int32), axis=1)).astype(jnp.int32)
    onehot = jnp.arange(VOL_GRP, dtype=jnp.int32)[:, None] == row_volume[None, :]
    row_level = (row_ids - lax.optimization_barrier(jnp.sum(jnp.where(onehot, starts[:, None], 0), axis=0))).astype(jnp.int32)
    return (row_volume, onehot.astype(jnp.float32), (row_volume * NBMAX + row_level).astype(jnp.int32))

def state_rows(state_slots, gather_index):
    shaped = state_slots.reshape(VOL_GRP, GPV_DEV, NBMAX, BS, 6)
    reordered = jnp.transpose(shaped, (0, 2, 3, 1, 4)).reshape(VOL_GRP * NBMAX, BS, GPV_DEV * 6)
    return reordered[gather_index]

def rows_state(row_values, gather_index):
    padded = jnp.zeros((VOL_GRP * NBMAX, BS, GPV_DEV * 6), row_values.dtype).at[gather_index].set(row_values)
    shaped = padded.reshape(VOL_GRP, NBMAX, BS, GPV_DEV, 6)
    return jnp.transpose(shaped, (0, 3, 1, 2, 4)).reshape(VOL_GRP * GPV_DEV, NBMAX * BS * 6)

def micro_solve(strain_slots, state_slots, vol_sizes, c_affine, coupling, diag_blk, diag_nrm, off_blk, off_rows, off_cols, off_nrm, live_count):
    row_volume, onehot, gather_index = row_layout(vol_sizes)
    strain_vg = strain_slots.astype(jnp.float32).reshape(VOL_GRP, GPV_DEV, 6)
    strain_rows = jnp.einsum('vr,vgk->rgk', onehot, strain_vg, precision=HIGHEST_PREC)
    diag_scale = 1.0 + GAIN_NORMAL * jnp.tanh(jnp.einsum('rk,rgk->rg', diag_nrm, strain_rows, precision=HIGHEST_PREC))
    diag_cols = jnp.repeat(diag_scale, 6, axis=1)
    off_strain = strain_vg[row_volume[off_rows]]
    live_mask = (jnp.arange(OFF_GRP, dtype=jnp.int32) < live_count).astype(jnp.float32)
    off_scale = (1.0 + GAIN_NORMAL * jnp.tanh(jnp.einsum('ok,ogk->og', off_nrm, off_strain, precision=HIGHEST_PREC))) * live_mask[:, None]
    off_scale_cols = jnp.repeat(off_scale, 6, axis=1)
    diag_vals = jnp.diagonal(diag_blk, axis1=1, axis2=2).astype(jnp.float32)
    load_rows = jnp.tile(jnp.swapaxes(coupling, 1, 2), (1, 1, GPV_DEV))
    denominator = diag_vals[:, :, None] * diag_cols[:, None, :]
    fluctuation = state_rows(state_slots, gather_index).astype(jnp.float32)
    diag_wide = diag_blk.astype(jnp.float32)
    off_wide = off_blk.astype(jnp.float32)
    for sweep_index in range(SWEEPS):
        fluct_low = fluctuation.astype(jnp.bfloat16)
        fluct_wide = fluct_low.astype(jnp.float32)
        applied = jnp.einsum('rab,rbc->rac', diag_wide, fluct_wide, precision=HIGHEST_PREC) * diag_cols[:, None, :]
        contact = jnp.einsum('oab,obc->oac', off_wide, fluct_wide[off_cols], precision=HIGHEST_PREC) * off_scale_cols[:, None, :]
        applied = applied.at[off_rows].add(contact)
        fluctuation = fluctuation + (load_rows - applied) / denominator
    projection = jnp.einsum('rid,rdc->ric', coupling, fluctuation, precision=HIGHEST_PREC)
    vol_proj = jnp.einsum('vr,ric->vic', onehot, projection, precision=HIGHEST_PREC)
    vol_proj = vol_proj / (vol_sizes.astype(jnp.float32) * BS)[:, None, None]
    tangent = c_affine.reshape(VOL_GRP, 6, 1, 6) - vol_proj.reshape(VOL_GRP, 6, GPV_DEV, 6)
    tangent = jnp.transpose(tangent, (0, 2, 1, 3)).reshape(VOL_GRP * GPV_DEV, 36).astype(jnp.bfloat16)
    state_new = rows_state(fluctuation.astype(jnp.bfloat16), gather_index)
    return (tangent, state_new)

def reference(displacement, nodal_load, connectivity, shape_grads, elem_volume, point_map, vol_blocks, c_affine, coupling, diag_blocks, diag_normal, off_blocks, off_row, off_col, off_normal, off_count, fluct_state):
    devices = N_SEC * N_BULK
    element_ids = jnp.arange(ELEMS, dtype=jnp.int32)
    node_ids = (connectivity + (element_ids // ELEM_DEV)[None, :] * NODE_DEV).astype(jnp.int32)
    strain = strain_of(shape_grads, displacement[:, node_ids])
    strain_sent = strain.T.astype(jnp.bfloat16)
    arrival_from = jnp.zeros((ELEMS,), jnp.int32).at[point_map].set(element_ids)

    def serve(state_pair, owner_id):
        tangent_all, fluct_all = state_pair
        group_id = owner_id % N_BULK
        members = lax.dynamic_slice_in_dim(arrival_from, owner_id * ELEM_DEV, ELEM_DEV)
        tangent, state_new = micro_solve(strain_sent[members], fluct_state[members], vol_blocks[group_id], c_affine[group_id], coupling[:, group_id], diag_blocks[:, group_id], diag_normal[:, group_id], off_blocks[:, group_id], off_row[:, group_id], off_col[:, group_id], off_normal[:, group_id], off_count[group_id])
        return ((tangent_all.at[members].set(tangent), fluct_all.at[members].set(state_new)), None)
    initial = (jnp.zeros((ELEMS, 36), jnp.bfloat16), jnp.zeros((ELEMS, NBMAX * BS * 6), jnp.bfloat16))
    scanned, unused = lax.scan(serve, initial, jnp.arange(devices, dtype=jnp.int32))
    tangent_all, fluct_new = scanned
    tangent_cols = tangent_all.astype(jnp.float32).T
    weights = elem_volume[None, :]
    stress = apply_tangent(tangent_cols, strain)
    residual = assemble(forces_of(shape_grads, weights * stress), node_ids, NODES) - nodal_load
    norm_sq = jnp.sum(residual * residual)
    root_mean = jnp.sqrt(norm_sq / (3.0 * NODES) + 1e-06)
    update = -jnp.minimum(1.0, CLIP_RMS / root_mean) * residual
    trial_strain = strain_of(shape_grads, residual[:, node_ids])
    product = assemble(forces_of(shape_grads, weights * apply_tangent(tangent_cols, trial_strain)), node_ids, NODES)
    return (residual, product, update, fluct_new)
```

```python
import jax
import jax.numpy as jnp
from jax import lax
from jax.experimental import pallas as pl
from jax.experimental.pallas import tpu as pltpu
from jax.sharding import PartitionSpec as P

F32 = jnp.float32
BF16 = jnp.bfloat16
I32 = jnp.int32
N_DEV = 128
ELEM = 512
NODE = 128
LEVEL = 768
MSG = 64
SWEEPS = 3
ROWS = 20
OFF = 32
MESH = pl.DeviceIdType.MESH
BASE = (0, 6, 18, 36)
SLOT0 = (0, 2, 6, 12)
STRIDE_PEER = 37


def dot_nt(a, b):
    return lax.dot_general(a, b, (((1,), (1,)), ((), ())), preferred_element_type=F32)


def dot_nn(a, b):
    return lax.dot_general(a, b, (((1,), (0,)), ((), ())), preferred_element_type=F32)


def iota(shape, dim):
    return lax.broadcasted_iota(I32, shape, dim)


def static_row(c, h, a):
    return SLOT0[c] + h * (c + 1) + a


def my_position():
    sec = lax.axis_index("sec")
    bulk = lax.axis_index("bulk")
    return sec, bulk, sec * 32 + bulk


def peer_of(step, sec, bulk):
    d = lax.rem(step * STRIDE_PEER, N_DEV)
    ty = lax.rem(sec + d // 32, 4)
    tx = lax.rem(bulk // 8 + lax.rem(d // 8, 4), 4)
    tz = lax.rem(lax.rem(bulk // 2, 4) + lax.rem(d // 2, 4), 4)
    tc = lax.rem(lax.rem(bulk, 2) + lax.rem(d, 2), 2)
    tb = (tx * 4 + tz) * 2 + tc
    return ty, tb, ty * 32 + tb


def greet_all(barrier, sec, bulk):
    def greet(step, carry):
        ty, tb, _ = peer_of(step, sec, bulk)
        pl.semaphore_signal(barrier, inc=1, device_id=(ty, tb), device_id_type=MESH)
        return carry

    lax.fori_loop(1, N_DEV, greet, 0)


def split3(nodal, scratch):
    high = nodal.astype(BF16).astype(F32)
    rest = nodal - high
    middle = rest.astype(BF16).astype(F32)
    low = rest - middle
    scratch[...] = jnp.zeros_like(scratch)
    rows = nodal.shape[0]
    scratch[0:rows, :] = high
    scratch[8 : 8 + rows, :] = middle
    scratch[16 : 16 + rows, :] = low
    return scratch[...].astype(BF16)


def node_onehot(conn_ref, a):
    ids = conn_ref[a : a + 1, :]
    return jnp.where(iota((NODE, ELEM), 0) == ids, 1.0, 0.0).astype(BF16)


def gather_nodes(nodal, conn_ref, scratch):
    parts = split3(nodal, scratch)
    out = []
    for a in range(4):
        got = dot_nn(parts, node_onehot(conn_ref, a))
        out.append(got[0:8] + got[8:16] + got[16:24])
    return out


def strain_rows(moved, grads_ref):
    g = [[grads_ref[3 * a + k : 3 * a + k + 1, :] for k in range(3)] for a in range(4)]
    u = [[moved[a][k : k + 1, :] for k in range(3)] for a in range(4)]

    def total(terms):
        out = terms[0]
        for t in terms[1:]:
            out = out + t
        return out

    return [
        total([g[a][0] * u[a][0] for a in range(4)]),
        total([g[a][1] * u[a][1] for a in range(4)]),
        total([g[a][2] * u[a][2] for a in range(4)]),
        total([g[a][2] * u[a][1] + g[a][1] * u[a][2] for a in range(4)]),
        total([g[a][2] * u[a][0] + g[a][0] * u[a][2] for a in range(4)]),
        total([g[a][1] * u[a][0] + g[a][0] * u[a][1] for a in range(4)]),
    ]


def make_spread(spread):
    m = iota((LEVEL, LEVEL), 0)
    n = iota((LEVEL, LEVEL), 1)
    spread[...] = jnp.where(m == lax.rem(n, 128) * 6 + n // 128, 1.0, 0.0).astype(BF16)


def pack_kernel(
    disp, conn, grads, pmap, state_hbm, got,
    state, stage, send, spread, srows, small, load_sem, own_sem, send_sem, recv_sem,
):
    sec, bulk, me = my_position()
    barrier = pltpu.get_barrier_semaphore()
    load = pltpu.make_async_copy(state_hbm, state, load_sem)
    load.start()
    greet_all(barrier, sec, bulk)

    strain = strain_rows(gather_nodes(disp[...], conn, small), grads)
    srows[...] = jnp.zeros_like(srows)
    for i in range(6):
        srows[i : i + 1, :] = strain[i]
    where_to = pmap[...]
    owner = where_to // ELEM
    volume = lax.rem(where_to, ELEM) // 64
    srows[8:9, :] = volume.astype(F32)
    strain_low = srows[...].astype(BF16)
    make_spread(spread)
    load.wait()

    ones = jnp.ones((16, LEVEL), BF16)
    levels = jnp.zeros((1, ELEM), I32)
    for a in range(4):
        weight = dot_nt(ones, jnp.abs(state[:, a * LEVEL : (a + 1) * LEVEL]))[0:1, :]
        levels = jnp.where(weight > 0.0, a + 1, levels)
    key = (owner * 4096 + levels * 512 + iota((1, ELEM), 1)).astype(F32)
    key_col = jnp.transpose(jnp.broadcast_to(key, (128, ELEM)))
    order = []
    for m in range(4):
        part = key[:, m * 128 : (m + 1) * 128]
        order.append(jnp.sum(jnp.where(key_col < part, 1.0, 0.0), axis=0, keepdims=True))
    order = jnp.concatenate(order, axis=1).astype(I32)

    for k in range(4):
        pick = jnp.where(order == iota((N_DEV, ELEM), 0) * 4 + k, 1.0, 0.0).astype(BF16)
        for a in range(k + 1):
            mine = dot_nn(pick, state[:, a * LEVEL : (a + 1) * LEVEL]).astype(BF16)
            flat = dot_nn(mine, spread[...])
            for j in range(6):
                stage[pl.ds(BASE[k] + a * 6 + j, N_DEV, stride=MSG), :] = flat[
                    :, j * 128 : (j + 1) * 128
                ]
        stage[pl.ds(60 + k, N_DEV, stride=MSG), :] = dot_nt(pick, strain_low)

    def lower(i, carry):
        send[pl.ds(i * 2, 2)] = (
            stage[pl.ds(pl.multiple_of(i * 2 * MSG, 2 * MSG), 2 * MSG), :]
            .astype(BF16)
            .reshape(2, MSG, 128)
        )
        return carry

    lax.fori_loop(0, N_DEV // 2, lower, 0)
    own = pltpu.make_async_copy(send.at[me], got.at[me], own_sem)
    own.start()
    pl.semaphore_wait(barrier, N_DEV - 1)

    def push(step, carry):
        ty, tb, t = peer_of(step, sec, bulk)
        pltpu.make_async_remote_copy(
            src_ref=send.at[t],
            dst_ref=got.at[me],
            send_sem=send_sem,
            recv_sem=recv_sem,
            device_id=(ty, tb),
            device_id_type=MESH,
        ).start()
        return carry

    lax.fori_loop(1, N_DEV, push, 0)
    own.wait()
    rest = send.at[pl.ds(0, N_DEV - 1)]
    pltpu.make_async_copy(rest, rest, send_sem).wait()
    landed = got.at[pl.ds(0, N_DEV - 1)]
    pltpu.make_async_copy(landed, landed, recv_sem).wait()


def solve_kernel(
    got, vols, coupling, diag, off, diag_n, off_n, off_row, off_col, off_count, affine,
    back,
    stage, state, low, chain, mask, strain, rdiag, cscale, dinv, weights, aff,
    vcls, ridx, inv, last, prev, ccol, cvol,
):
    start = jnp.int32(0)
    seen = [jnp.int32(0)] * 4
    for v in range(8):
        nb = vols[0, v]
        half = jnp.int32(0)
        for c in range(4):
            half = jnp.where(nb == c + 1, seen[c], half)
            seen[c] = seen[c] + jnp.where(nb == c + 1, 1, 0)
        vcls[(nb - 1) * 2 + half] = v
        for a in range(4):
            slot = (nb - 1) * nb + half * nb + a

            @pl.when(a < nb)
            def _():
                ridx[slot] = start + a
                inv[start + a] = slot
                last[slot] = 0

        cvol_id = (nb - 1) * 2 + half
        start = start + nb
        for a in range(4):
            pass
        vcls[8 + v] = cvol_id
    for c in range(4):
        for h in range(2):
            for a in range(c + 1):
                vcls[16 + static_row(c, h, a)] = c * 2 + h

    def link(c, carry):
        row = inv[off_row[c, 0]]
        ccol[c] = inv[off_col[c, 0]]
        cvol[c] = vcls[16 + row]
        prev[c] = last[row]
        last[row] = c + 1
        return carry

    lax.fori_loop(0, OFF, link, 0)

    lanes6 = iota((36, 128), 1)
    rows6 = iota((36, 128), 0)
    place = jnp.where(
        lanes6 == lax.rem(rows6, 6) * 8 + rows6 // 6, 1.0, 0.0
    ).astype(F32)
    aff[...] = lax.dot_general(
        affine[0], place, (((1,), (0,)), ((), ())),
        preferred_element_type=F32, precision=lax.Precision.HIGHEST,
    )
    eye = iota((128, 128), 0) == iota((128, 128), 1)

    def prepare(i, carry):
        r = ridx[i]
        values = jnp.where(eye, diag[r].astype(F32), 0.0)
        dinv[i] = 1.0 / jnp.sum(values, axis=0, keepdims=True)
        load = coupling[r]
        high = load.astype(BF16).astype(F32)
        block = jnp.zeros((58, 128), F32)
        weights[i] = jnp.concatenate([high, block, load - high, block], axis=0).astype(BF16)
        return carry

    lax.fori_loop(0, ROWS, prepare, 0)
    chain[0] = jnp.zeros((192, 128), F32)
    live = off_count[0]

    def phase(p, carry):
        def widen(i, c2):
            stage[pl.ds(pl.multiple_of(i * MSG, MSG), MSG), :] = got[2 * i + p].astype(F32)
            return c2

        lax.fori_loop(0, 64, widen, 0, unroll=2)
        tail = [stage[pl.ds(60 + k, 64, stride=MSG), :] for k in range(4)]
        for c in range(4):
            for h in range(2):
                v = vcls[c * 2 + h].astype(F32)
                picked = jnp.zeros((32, 128), F32)
                for k in range(4):
                    part = tail[k][h * 32 : (h + 1) * 32]
                    m = jnp.where(jnp.broadcast_to(part[:, 8:9], (32, 128)) == v, 1.0, 0.0)
                    mask[(c * 2 + h) * 4 + k] = m
                    picked = picked + m * part
                for i in range(6):
                    strain[(c * 2 + h) * 6 + i] = jnp.broadcast_to(picked[:, i : i + 1], (32, 128))
        for h in range(2):
            for a in range(4):
                for j in range(6):
                    sums = {}
                    for k in range(a, 4):
                        part = stage[pl.ds(h * 32 * MSG + BASE[k] + a * 6 + j, 32, stride=MSG), :]
                        for c in range(a, 4):
                            term = mask[(c * 2 + h) * 4 + k] * part
                            sums[c] = sums[c] + term if c in sums else term
                    for c in range(a, 4):
                        i = static_row(c, h, a)
                        state[i, j * 32 : (j + 1) * 32, :] = sums[c]
                        low[i, j * 32 : (j + 1) * 32, :] = sums[c].astype(BF16)

        def row_scale(i, c2):
            r = ridx[i]
            ch = vcls[16 + i]
            z = diag_n[r, 0, 0] * strain[ch * 6]
            for k in range(1, 6):
                z = z + diag_n[r, 0, k] * strain[ch * 6 + k]
            rdiag[i] = 1.0 / (1.0 + 0.4 * jnp.tanh(z))
            return c2

        lax.fori_loop(0, ROWS, row_scale, 0, unroll=4)

        def contact_scale(c, c2):
            ch = cvol[c]
            z = off_n[c, 0, 0] * strain[ch * 6]
            for k in range(1, 6):
                z = z + off_n[c, 0, k] * strain[ch * 6 + k]
            on = jnp.where(c < live, 1.0, 0.0).astype(F32)
            cscale[c] = (1.0 + 0.4 * jnp.tanh(z)) * on
            return c2

        lax.fori_loop(0, OFF, contact_scale, 0, unroll=4)

        def sweep(n, c2):
            def contact(c, c3):
                value = dot_nt(low[ccol[c]], off[c]).reshape(6, 32, 128)
                scaled = (value * cscale[c][None]).reshape(192, 128)
                chain[c + 1] = chain[prev[c]] + scaled
                return c3

            lax.fori_loop(0, OFF, contact, 0, unroll=4)

            def update(i, c3):
                r = ridx[i]
                own = dot_nt(low[i], diag[r]).reshape(6, 32, 128)
                extra = chain[last[i]].reshape(6, 32, 128)
                step = ((coupling[r][:, None, :] - extra) * rdiag[i][None] - own) * dinv[i][None]
                new = state[i] + step.reshape(192, 128)
                state[i] = new
                low[i] = new.astype(BF16)
                return c3

            lax.fori_loop(0, ROWS, update, 0, unroll=4)
            return c2

        lax.fori_loop(0, SWEEPS, sweep, 0)

        lane = iota((32, 128), 1)
        for c in range(4):
            for h in range(2):
                acc = jnp.zeros((192, 128), F32)
                for a in range(c + 1):
                    i = static_row(c, h, a)
                    x = state[i]
                    high = low[i]
                    acc = acc + dot_nt(high, weights[i])
                    acc = acc + dot_nt((x - high.astype(F32)).astype(BF16), weights[i])
                    for j in range(6):
                        stage[pl.ds(h * 32 * MSG + BASE[c] + a * 6 + j, 32, stride=MSG), :] = x[
                            j * 32 : (j + 1) * 32
                        ]
                t = acc[0:32]
                for j in range(1, 6):
                    t = t + pltpu.roll(acc[j * 32 : (j + 1) * 32], 8 * j, axis=1)
                t = t + pltpu.roll(t, 64, axis=1)
                v = vcls[c * 2 + h]
                tangent = aff[pl.ds(v, 1), :] - t / (128.0 * (c + 1))
                row = jnp.where(lane < 48, tangent, jnp.where(lane == 64, v.astype(F32), 0.0))
                stage[pl.ds(h * 32 * MSG + 60 + c, 32, stride=MSG), :] = row

        def lower(i, c2):
            back[2 * i + p] = stage[pl.ds(pl.multiple_of(i * MSG, MSG), MSG), :].astype(BF16)
            return c2

        lax.fori_loop(0, 64, lower, 0, unroll=2)
        return carry

    lax.fori_loop(0, 2, phase, 0)


def forces_of(grads_ref, s):
    g = [[grads_ref[3 * a + k : 3 * a + k + 1, :] for k in range(3)] for a in range(4)]
    out = []
    for a in range(4):
        gx, gy, gz = g[a]
        out.append(
            (
                gx * s[0] + gz * s[4] + gy * s[5],
                gy * s[1] + gz * s[3] + gx * s[5],
                gz * s[2] + gy * s[3] + gx * s[4],
            )
        )
    return out


def assemble(grads_ref, conn_ref, stress, scratch):
    forces = forces_of(grads_ref, stress)
    total = jnp.zeros((8, NODE), F32)
    for a in range(4):
        scratch[...] = jnp.zeros_like(scratch)
        for k in range(3):
            f = forces[a][k]
            high = f.astype(BF16).astype(F32)
            rest = f - high
            middle = rest.astype(BF16).astype(F32)
            scratch[k : k + 1, :] = high
            scratch[8 + k : 9 + k, :] = middle
            scratch[16 + k : 17 + k, :] = rest - middle
        part = dot_nt(scratch[...].astype(BF16), node_onehot(conn_ref, a))
        total = total + (part[0:8] + part[8:16] + part[16:24])
    return total[0:3]


def apply_tangent(tangent, strain, weight):
    acc = tangent[0:8] * strain[0]
    for j in range(1, 6):
        acc = acc + tangent[8 * j : 8 * j + 8] * strain[j]
    acc = acc * weight
    return [acc[i : i + 1, :] for i in range(6)]


def home_kernel(
    send, disp, load_ref, conn, grads, volume_ref, pmap,
    tail, body, residual_ref, product_ref, update_ref,
    tails, wide, small, small_e, mine, norms,
    own_sems, tail_send, tail_recv, body_send, body_recv, norm_send, norm_recv,
):
    sec, bulk, me = my_position()
    barrier = pltpu.get_barrier_semaphore()
    greet_all(barrier, sec, bulk)
    own_tail = pltpu.make_async_copy(send.at[me, pl.ds(48, 16)], tails.at[me], own_sems.at[0])
    own_body = pltpu.make_async_copy(send.at[me, pl.ds(0, 48)], body.at[me], own_sems.at[1])
    own_tail.start()
    own_body.start()
    pl.semaphore_wait(barrier, N_DEV - 1)

    def push_tail(step, carry):
        ty, tb, t = peer_of(step, sec, bulk)
        pltpu.make_async_remote_copy(
            src_ref=send.at[t, pl.ds(48, 16)],
            dst_ref=tails.at[me],
            send_sem=tail_send,
            recv_sem=tail_recv,
            device_id=(ty, tb),
            device_id_type=MESH,
        ).start()
        return carry

    def push_body(step, carry):
        ty, tb, t = peer_of(step, sec, bulk)
        pltpu.make_async_remote_copy(
            src_ref=send.at[t, pl.ds(0, 48)],
            dst_ref=body.at[me],
            send_sem=body_send,
            recv_sem=body_recv,
            device_id=(ty, tb),
            device_id_type=MESH,
        ).start()
        return carry

    lax.fori_loop(1, N_DEV, push_tail, 0)
    lax.fori_loop(1, N_DEV, push_body, 0)

    strain = strain_rows(gather_nodes(disp[...], conn, small), grads)
    where_to = pmap[...]
    owner = where_to // ELEM
    volume = (lax.rem(where_to, ELEM) // 64).astype(F32)
    same_owner = iota((N_DEV, ELEM), 0) == owner

    own_tail.wait()
    landed = tails.at[pl.ds(0, N_DEV - 1)]
    pltpu.make_async_copy(landed, landed, tail_recv).wait()
    wide[...] = tails[...].astype(F32).reshape(N_DEV * 16, 128)
    keep = pltpu.make_async_copy(tails, tail, own_sems.at[2])
    keep.start()
    tangent = jnp.zeros((128, ELEM), F32)
    for c in range(4):
        part = wide[pl.ds(12 + c, N_DEV, stride=16), :]
        code = jnp.broadcast_to(part[:, 64:65], (N_DEV, ELEM))
        pick = jnp.where(same_owner & (code == volume), 1.0, 0.0).astype(BF16)
        tangent = tangent + dot_nn(jnp.transpose(part).astype(BF16), pick)
    weight = volume_ref[...]
    residual = (
        assemble(grads, conn, apply_tangent(tangent, strain, weight), small_e) - load_ref[...]
    )
    residual_ref[...] = residual
    mine[...] = jnp.broadcast_to(
        jnp.sum(jnp.sum(residual * residual, axis=1, keepdims=True), axis=0, keepdims=True),
        (8, 128),
    )
    norms[me] = mine[...]

    def push_norm(step, carry):
        ty, tb, t = peer_of(step, sec, bulk)
        pltpu.make_async_remote_copy(
            src_ref=mine,
            dst_ref=norms.at[me],
            send_sem=norm_send,
            recv_sem=norm_recv,
            device_id=(ty, tb),
            device_id_type=MESH,
        ).start()
        return carry

    lax.fori_loop(1, N_DEV, push_norm, 0)
    trial = strain_rows(gather_nodes(residual, conn, small), grads)
    product_ref[...] = assemble(grads, conn, apply_tangent(tangent, trial, weight), small_e)
    arrived = norms.at[pl.ds(0, N_DEV - 1)]
    pltpu.make_async_copy(arrived, arrived, norm_recv).wait()
    total = jnp.sum(norms[...], axis=0)[0:1, :]
    root = jnp.sqrt(total / (3.0 * 16384) + 1e-06)
    update_ref[...] = -jnp.minimum(1.0, 1.0 / root) * residual

    pltpu.make_async_copy(arrived, arrived, norm_send).wait()
    keep.wait()
    own_body.wait()
    pltpu.make_async_copy(landed, landed, tail_send).wait()
    rest = body.at[pl.ds(0, N_DEV - 1)]
    pltpu.make_async_copy(rest, rest, body_send).wait()
    pltpu.make_async_copy(rest, rest, body_recv).wait()


def unpack_kernel(tail, body, pmap, out_hbm, stage, spread, flat, result, sems):
    make_spread(spread)

    def widen(i, carry):
        at = pl.multiple_of(i * MSG, MSG)
        stage[pl.ds(at, 48), :] = body[i].astype(F32)
        stage[pl.ds(at + 48, 16), :] = tail[i].astype(F32)
        return carry

    lax.fori_loop(0, N_DEV, widen, 0, unroll=2)
    where_to = pmap[...].astype(F32)
    column = jnp.transpose(jnp.broadcast_to(where_to, (128, ELEM))).astype(I32)
    owner = column // ELEM
    volume = lax.rem(column, ELEM) // 64
    same_owner = iota((ELEM, N_DEV), 1) == owner
    picks = []
    for c in range(4):
        part = stage[pl.ds(60 + c, N_DEV, stride=MSG), :]
        code = jnp.transpose(part)[64:65, :].astype(I32)
        picks.append(jnp.where(same_owner & (code == volume), 1.0, 0.0).astype(BF16))
    pick = jnp.concatenate(picks, axis=1)
    copies = []
    for a in range(4):
        for c in range(a, 4):
            row = jnp.concatenate(
                [
                    stage[pl.ds(BASE[c] + a * 6 + j, N_DEV, stride=MSG), :].astype(BF16)
                    for j in range(6)
                ],
                axis=1,
            )
            flat[c * 128 : (c + 1) * 128, :] = dot_nt(row, spread[...]).astype(BF16)
        result[:, a * LEVEL : (a + 1) * LEVEL] = dot_nn(
            pick[:, a * 128 :], flat[a * 128 :, :]
        ).astype(BF16)
        part = pl.ds(a * LEVEL, LEVEL)
        copy = pltpu.make_async_copy(result.at[:, part], out_hbm.at[:, part], sems.at[a])
        copy.start()
        copies.append(copy)
    for copy in copies:
        copy.wait()


VMEM = pl.BlockSpec(memory_space=pltpu.VMEM)
SMEM = pl.BlockSpec(memory_space=pltpu.SMEM)
ANY = pl.BlockSpec(memory_space=pl.ANY)
DMA = pltpu.SemaphoreType.DMA


def params(collective_id=None, limit=48):
    return pltpu.CompilerParams(
        collective_id=collective_id,
        has_side_effects=collective_id is not None,
        vmem_limit_bytes=limit * 2**20,
    )


def on_device(
    displacement, nodal_load, connectivity, shape_grads, elem_volume, point_map, vol_blocks,
    c_affine, coupling, diag_blocks, diag_normal, off_blocks, off_row, off_col, off_normal,
    off_count, fluct_state,
):
    pmap = point_map.reshape(1, ELEM)
    volume = elem_volume.reshape(1, ELEM)
    got = pl.pallas_call(
        pack_kernel,
        out_shape=jax.ShapeDtypeStruct((N_DEV, MSG, 128), BF16),
        in_specs=[VMEM, VMEM, VMEM, VMEM, ANY],
        out_specs=ANY,
        scratch_shapes=[
            pltpu.VMEM((ELEM, 4 * LEVEL), BF16),
            pltpu.VMEM((N_DEV * MSG, 128), F32),
            pltpu.VMEM((N_DEV, MSG, 128), BF16),
            pltpu.VMEM((LEVEL, LEVEL), BF16),
            pltpu.VMEM((128, ELEM), F32),
            pltpu.VMEM((32, 128), F32),
            DMA, DMA, DMA, DMA,
        ],
        compiler_params=params(1),
        name="pack",
    )(displacement, connectivity, shape_grads, pmap, fluct_state)
    smem = lambda n: pltpu.SMEM((n,), I32)
    back = pl.pallas_call(
        solve_kernel,
        out_shape=jax.ShapeDtypeStruct((N_DEV, MSG, 128), BF16),
        in_specs=[VMEM, SMEM, VMEM, VMEM, VMEM, SMEM, SMEM, SMEM, SMEM, SMEM, VMEM],
        out_specs=VMEM,
        scratch_shapes=[
            pltpu.VMEM((64 * MSG, 128), F32),
            pltpu.VMEM((ROWS, 192, 128), F32),
            pltpu.VMEM((ROWS, 192, 128), BF16),
            pltpu.VMEM((OFF + 1, 192, 128), F32),
            pltpu.VMEM((32, 32, 128), F32),
            pltpu.VMEM((48, 32, 128), F32),
            pltpu.VMEM((ROWS, 32, 128), F32),
            pltpu.VMEM((OFF, 32, 128), F32),
            pltpu.VMEM((ROWS, 1, 128), F32),
            pltpu.VMEM((ROWS, 128, 128), BF16),
            pltpu.VMEM((8, 128), F32),
            smem(36), smem(ROWS), smem(ROWS), smem(ROWS), smem(OFF), smem(OFF), smem(OFF),
        ],
        compiler_params=params(),
        name="solve",
    )(
        got, vol_blocks, coupling[:, 0], diag_blocks[:, 0], off_blocks[:, 0], diag_normal,
        off_normal, off_row, off_col, off_count, c_affine,
    )
    nodal = jax.ShapeDtypeStruct((3, NODE), F32)
    tail, body, residual, product, update = pl.pallas_call(
        home_kernel,
        out_shape=(
            jax.ShapeDtypeStruct((N_DEV, 16, 128), BF16),
            jax.ShapeDtypeStruct((N_DEV, 48, 128), BF16),
            nodal, nodal, nodal,
        ),
        in_specs=[VMEM] * 7,
        out_specs=(ANY, ANY, VMEM, VMEM, VMEM),
        scratch_shapes=[
            pltpu.VMEM((N_DEV, 16, 128), BF16),
            pltpu.VMEM((N_DEV * 16, 128), F32),
            pltpu.VMEM((32, 128), F32),
            pltpu.VMEM((32, ELEM), F32),
            pltpu.VMEM((8, 128), F32),
            pltpu.VMEM((N_DEV, 8, 128), F32),
            pltpu.SemaphoreType.DMA((3,)),
            DMA, DMA, DMA, DMA, DMA, DMA,
        ],
        compiler_params=params(2),
        name="home",
    )(back, displacement, nodal_load, connectivity, shape_grads, volume, pmap)
    fluct_new = pl.pallas_call(
        unpack_kernel,
        out_shape=jax.ShapeDtypeStruct((ELEM, 4 * LEVEL), BF16),
        in_specs=[VMEM, VMEM, VMEM],
        out_specs=ANY,
        scratch_shapes=[
            pltpu.VMEM((N_DEV * MSG, 128), F32),
            pltpu.VMEM((LEVEL, LEVEL), BF16),
            pltpu.VMEM((512, LEVEL), BF16),
            pltpu.VMEM((ELEM, 4 * LEVEL), BF16),
            pltpu.SemaphoreType.DMA((4,)),
        ],
        compiler_params=params(),
        name="unpack",
    )(tail, body, pmap)
    return residual, product, update, fluct_new


def solution(mesh):
    both = ("sec", "bulk")
    return jax.shard_map(
        on_device,
        mesh=mesh,
        in_specs=(
            P(None, both), P(None, both), P(None, both), P(None, both), P(both), P(both),
            P("bulk", None), P("bulk", None, None), P(None, "bulk", None, None),
            P(None, "bulk", None, None), P(None, "bulk", None), P(None, "bulk", None, None),
            P(None, "bulk"), P(None, "bulk"), P(None, "bulk", None), P("bulk"), P(both, None),
        ),
        out_specs=(P(None, both), P(None, both), P(None, both), P(both, None)),
        check_vma=False,
    )
```

```python
import jax
import jax.numpy as jnp
from jax import lax
from jax.experimental import pallas as pl
from jax.experimental.pallas import tpu as pltpu
from jax.sharding import PartitionSpec as P

F32 = jnp.float32
BF16 = jnp.bfloat16
I32 = jnp.int32
N_DEV = 128
ELEM = 512
NODE = 128
LEVEL = 768
MSG = 64
SWEEPS = 3
ROWS = 20
OFF = 32
MESH = pl.DeviceIdType.MESH
BASE = (0, 6, 18, 36)
SLOT0 = (0, 2, 6, 12)
STRIDE_PEER = 37
STRIDE_CHIP = 27
DELAY = True


def dot_nt(a, b):
    return lax.dot_general(a, b, (((1,), (1,)), ((), ())), preferred_element_type=F32)


def dot_nn(a, b):
    return lax.dot_general(a, b, (((1,), (0,)), ((), ())), preferred_element_type=F32)


def iota(shape, dim):
    return lax.broadcasted_iota(I32, shape, dim)


def static_row(c, h, a):
    return SLOT0[c] + h * (c + 1) + a


def my_position():
    sec = lax.axis_index("sec")
    bulk = lax.axis_index("bulk")
    return sec, bulk, sec * 32 + bulk


def peer_of(step, sec, bulk):
    d = lax.rem(step * STRIDE_PEER, N_DEV)
    ty = lax.rem(sec + d // 32, 4)
    tx = lax.rem(bulk // 8 + lax.rem(d // 8, 4), 4)
    tz = lax.rem(lax.rem(bulk // 2, 4) + lax.rem(d // 2, 4), 4)
    tc = lax.rem(lax.rem(bulk, 2) + lax.rem(d, 2), 2)
    tb = (tx * 4 + tz) * 2 + tc
    return ty, tb, ty * 32 + tb


def chip_peer(step, core, sec, bulk):
    d = lax.rem(step * STRIDE_CHIP, N_DEV // 2)
    ty = lax.rem(sec + d // 16, 4)
    tx = lax.rem(bulk // 8 + lax.rem(d // 4, 4), 4)
    tz = lax.rem(lax.rem(bulk // 2, 4) + lax.rem(d, 4), 4)
    tb = (tx * 4 + tz) * 2 + core
    return ty, tb, ty * 32 + tb


def greet_all(barrier, sec, bulk):
    def greet(step, carry):
        ty, tb, _ = peer_of(step, sec, bulk)
        pl.semaphore_signal(barrier, inc=1, device_id=(ty, tb), device_id_type=MESH)
        return carry

    lax.fori_loop(1, N_DEV, greet, 0)


def split3(nodal, scratch):
    high = nodal.astype(BF16).astype(F32)
    rest = nodal - high
    middle = rest.astype(BF16).astype(F32)
    low = rest - middle
    scratch[...] = jnp.zeros_like(scratch)
    rows = nodal.shape[0]
    scratch[0:rows, :] = high
    scratch[8 : 8 + rows, :] = middle
    scratch[16 : 16 + rows, :] = low
    return scratch[...].astype(BF16)


def node_onehot(conn_ref, a):
    ids = conn_ref[a : a + 1, :]
    return jnp.where(iota((NODE, ELEM), 0) == ids, 1.0, 0.0).astype(BF16)


def gather_nodes(nodal, conn_ref, scratch):
    parts = split3(nodal, scratch)
    out = []
    for a in range(4):
        got = dot_nn(parts, node_onehot(conn_ref, a))
        out.append(got[0:8] + got[8:16] + got[16:24])
    return out


def strain_rows(moved, grads_ref):
    g = [[grads_ref[3 * a + k : 3 * a + k + 1, :] for k in range(3)] for a in range(4)]
    u = [[moved[a][k : k + 1, :] for k in range(3)] for a in range(4)]

    def total(terms):
        out = terms[0]
        for t in terms[1:]:
            out = out + t
        return out

    return [
        total([g[a][0] * u[a][0] for a in range(4)]),
        total([g[a][1] * u[a][1] for a in range(4)]),
        total([g[a][2] * u[a][2] for a in range(4)]),
        total([g[a][2] * u[a][1] + g[a][1] * u[a][2] for a in range(4)]),
        total([g[a][2] * u[a][0] + g[a][0] * u[a][2] for a in range(4)]),
        total([g[a][1] * u[a][0] + g[a][0] * u[a][1] for a in range(4)]),
    ]


def make_spread(spread):
    n = iota((1, LEVEL), 1)
    source = lax.rem(n, 128) * 6 + n // 128
    spread[...] = jnp.where(iota((LEVEL, LEVEL), 0) == source, 1.0, 0.0).astype(BF16)


def prepare_send(strain, pmap, state, stage, send, spread, flat, srows, load):
    srows[...] = jnp.zeros_like(srows)
    for i in range(6):
        srows[i : i + 1, :] = strain[i]
    where_to = pmap[...]
    owner = where_to // ELEM
    volume = lax.rem(where_to, ELEM) // 64
    srows[8:9, :] = volume.astype(F32)
    strain_low = srows[...].astype(BF16)
    make_spread(spread)
    load.wait()

    ones = jnp.ones((16, LEVEL), BF16)
    levels = jnp.zeros((1, ELEM), I32)
    for a in range(4):
        weight = dot_nt(ones, jnp.abs(state[:, a * LEVEL : (a + 1) * LEVEL]))[0:1, :]
        levels = jnp.where(weight > 0.0, a + 1, levels)
    key = (owner * 4096 + levels * 512 + iota((1, ELEM), 1)).astype(F32)
    key_col = jnp.transpose(jnp.broadcast_to(key, (128, ELEM)))
    order = []
    for m in range(4):
        part = key[:, m * 128 : (m + 1) * 128]
        order.append(jnp.sum(jnp.where(key_col < part, 1.0, 0.0), axis=0, keepdims=True))
    order = jnp.concatenate(order, axis=1).astype(I32)

    at = 0
    for k in range(4):
        pick = jnp.where(order == iota((N_DEV, ELEM), 0) * 4 + k, 1.0, 0.0).astype(BF16)
        for a in range(k + 1):
            mine = dot_nn(pick, state[:, a * LEVEL : (a + 1) * LEVEL])
            flat[at * 128 : (at + 1) * 128, :] = mine.astype(BF16)
            at += 1
        stage[pl.ds(60 + k, N_DEV, stride=MSG), :] = dot_nt(pick, strain_low)
    for jj in range(3):
        for half in range(2):
            got = dot_nn(
                flat[half * 640 : (half + 1) * 640, :], spread[:, jj * 256 : (jj + 1) * 256]
            )
            for i in range(5):
                at = half * 5 + i
                for j in range(2):
                    stage[pl.ds(at * 6 + jj * 2 + j, N_DEV, stride=MSG), :] = got[
                        i * 128 : (i + 1) * 128, j * 128 : (j + 1) * 128
                    ]

    def lower(i, carry):
        at = pl.multiple_of(i * 2 * MSG, 2 * MSG)
        send[pl.ds(i * 2, 2)] = (
            stage[pl.ds(at, 2 * MSG), :].astype(BF16).reshape(2, MSG, 128)
        )
        return carry

    lax.fori_loop(0, N_DEV // 2, lower, 0, unroll=4)


def make_tables(vols, off_row, off_col, vcls, chrow, ridx, inv, last, prev, crow, ccol, cvol):
    sizes = [vols[0, v] for v in range(8)]
    zero = jnp.int32(0)
    halves, starts, start = [], [], zero
    for v in range(8):
        half = zero
        for w in range(v):
            half = half + jnp.where(sizes[w] == sizes[v], 1, 0)
        halves.append(half)
        starts.append(start)
        start = start + sizes[v]
    for c in range(4):
        for h in range(2):
            vol, first = zero, zero
            for v in range(8):
                hit = (sizes[v] == c + 1) & (halves[v] == h)
                vol = jnp.where(hit, v, vol)
                first = jnp.where(hit, starts[v], first)
            vcls[c * 2 + h] = vol
            for a in range(c + 1):
                ridx[static_row(c, h, a)] = first + a
                chrow[static_row(c, h, a)] = c * 2 + h

    def invert(r, carry):
        found = jnp.int32(0)
        for i in range(ROWS):
            found = jnp.where(ridx[i] == r, i, found)
        inv[r] = found
        return carry

    lax.fori_loop(0, ROWS, invert, 0)

    def ends(c, carry):
        row = inv[off_row[0, c]]
        crow[c] = row
        ccol[c] = inv[off_col[0, c]]
        cvol[c] = chrow[row]
        return carry

    lax.fori_loop(0, OFF, ends, 0)

    def link(c, carry):
        row = crow[c]
        before = jnp.int32(0)
        for k in range(OFF):
            before = jnp.where((crow[k] == row) & (k < c), k + 1, before)
        prev[c] = before
        return carry

    lax.fori_loop(0, OFF, link, 0)

    def finish(i, carry):
        end = jnp.int32(0)
        for k in range(OFF):
            end = jnp.where(crow[k] == i, k + 1, end)
        last[i] = end
        return carry

    lax.fori_loop(0, ROWS, finish, 0)


def step_kernel(
    disp, load_ref, conn, grads, volume_ref, pmap, vols, affine, diag_n, off_n, off_row,
    off_col, off_count, coupling_hbm, diag_hbm, off_hbm, state_hbm,
    tail, body, residual_ref, product_ref, update_ref,
    fluct, stage, send, spread, flat, srows, small, small_e,
    got, back, coupling, diag, off,
    state, low, chain, mask, strain, rdiag, cscale, dinv, weights, aff,
    tails, wide, mine, norms,
    vcls, chrow, ridx, inv, last, prev, crow, ccol, cvol,
    load_sems, own_sems, go_send, go_recv, tail_send, tail_recv, body_send, body_recv,
    norm_send, norm_recv,
):
    sec, bulk, me = my_position()
    core = lax.rem(bulk, 2)
    barrier = pltpu.get_barrier_semaphore()
    loads = []
    for i, (source, target) in enumerate(
        [(state_hbm, fluct), (off_hbm, off), (diag_hbm, diag), (coupling_hbm, coupling)]
    ):
        loads.append(pltpu.make_async_copy(source, target, load_sems.at[i]))
        loads[-1].start()
    greet_all(barrier, sec, bulk)
    macro = strain_rows(gather_nodes(disp[...], conn, small), grads)
    prepare_send(macro, pmap, fluct, stage, send, spread, flat, srows, loads[0])
    own = pltpu.make_async_copy(send.at[me], got.at[core, me // 2], own_sems.at[0])
    own.start()
    pl.semaphore_wait(barrier, N_DEV - 1)

    def push(step, carry):
        ty, tb, t = peer_of(step, sec, bulk)
        pltpu.make_async_remote_copy(
            src_ref=send.at[t],
            dst_ref=got.at[core, me // 2],
            send_sem=go_send,
            recv_sem=go_recv.at[core],
            device_id=(ty, tb),
            device_id_type=MESH,
        ).start()
        return carry

    if DELAY:

        @pl.when(core == 0)
        def _():
            lax.fori_loop(1, N_DEV, push, 0)

    else:
        lax.fori_loop(1, N_DEV, push, 0)

    make_tables(vols, off_row, off_col, vcls, chrow, ridx, inv, last, prev, crow, ccol, cvol)
    lanes6 = iota((36, 128), 1)
    rows6 = iota((36, 128), 0)
    place = jnp.where(lanes6 == lax.rem(rows6, 6) * 8 + rows6 // 6, 1.0, 0.0).astype(F32)
    spread_affine = lax.dot_general(
        affine[0], place, (((1,), (0,)), ((), ())),
        preferred_element_type=F32, precision=lax.Precision.HIGHEST,
    )
    for v in range(8):
        aff[v] = spread_affine[v : v + 1, :]
    eye = iota((128, 128), 0) == iota((128, 128), 1)
    for load in loads[1:]:
        load.wait()

    def prepare(i, carry):
        r = ridx[i]
        values = jnp.where(eye, diag[r].astype(F32), 0.0)
        dinv[i] = 1.0 / jnp.sum(values, axis=0, keepdims=True)
        load = coupling[r].reshape(6, 128)
        high = load.astype(BF16).astype(F32)
        block = jnp.zeros((58, 128), F32)
        weights[i] = jnp.concatenate([high, block, load - high, block], axis=0).astype(BF16)
        return carry

    lax.fori_loop(0, ROWS, prepare, 0, unroll=2)
    chain[0] = jnp.zeros((192, 128), F32)
    live = off_count[0]
    own.wait()

    def phase(p, carry):
        @pl.when(core == p)
        def _():
            part = got.at[p, pl.ds(0, 63)]
            pltpu.make_async_copy(part, part, go_recv.at[p]).wait()

        @pl.when(core != p)
        def _():
            part = got.at[p]
            pltpu.make_async_copy(part, part, go_recv.at[p]).wait()

        if DELAY:

            @pl.when((p == 0) & (core == 1))
            def _():
                lax.fori_loop(1, N_DEV, push, 0)

        def widen(i, c2):
            at = pl.multiple_of(i * 2 * MSG, 2 * MSG)
            stage[pl.ds(at, 2 * MSG), :] = (
                got[p, pl.ds(2 * i, 2)].astype(F32).reshape(2 * MSG, 128)
            )
            return c2

        lax.fori_loop(0, 32, widen, 0, unroll=4)
        rest = [stage[pl.ds(60 + k, 64, stride=MSG), :] for k in range(4)]
        for c in range(4):
            for h in range(2):
                v = vcls[c * 2 + h].astype(F32)
                picked = jnp.zeros((32, 128), F32)
                for k in range(4):
                    part = rest[k][h * 32 : (h + 1) * 32]
                    m = jnp.where(jnp.broadcast_to(part[:, 8:9], (32, 128)) == v, 1.0, 0.0)
                    mask[(c * 2 + h) * 4 + k] = m
                    picked = picked + m * part
                for i in range(6):
                    strain[(c * 2 + h) * 6 + i] = jnp.broadcast_to(picked[:, i : i + 1], (32, 128))
        for h in range(2):
            for a in range(4):
                for j in range(6):
                    sums = {}
                    for k in range(a, 4):
                        part = stage[pl.ds(h * 32 * MSG + BASE[k] + a * 6 + j, 32, stride=MSG), :]
                        for c in range(a, 4):
                            term = mask[(c * 2 + h) * 4 + k] * part
                            sums[c] = sums[c] + term if c in sums else term
                    for c in range(a, 4):
                        i = static_row(c, h, a)
                        state[i, j * 32 : (j + 1) * 32, :] = sums[c]
                        low[i, j * 32 : (j + 1) * 32, :] = sums[c].astype(BF16)

        def row_scale(i, c2):
            r = ridx[i]
            ch = chrow[i] * 6
            z = diag_n[0, 0, r] * strain[ch]
            for k in range(1, 6):
                z = z + diag_n[k, 0, r] * strain[ch + k]
            rdiag[i] = 1.0 / (1.0 + 0.4 * jnp.tanh(z))
            return c2

        lax.fori_loop(0, ROWS, row_scale, 0, unroll=5)

        def contact_scale(c, c2):
            ch = cvol[c] * 6
            z = off_n[0, 0, c] * strain[ch]
            for k in range(1, 6):
                z = z + off_n[k, 0, c] * strain[ch + k]
            on = jnp.where(c < live, 1.0, 0.0).astype(F32)
            cscale[c] = (1.0 + 0.4 * jnp.tanh(z)) * on
            return c2

        lax.fori_loop(0, OFF, contact_scale, 0, unroll=8)

        def sweep(n, c2):
            def contact(c, c3):
                value = dot_nt(low[ccol[c]], off[c]).reshape(6, 32, 128)
                scaled = (value * cscale[c][None]).reshape(192, 128)
                chain[c + 1] = chain[prev[c]] + scaled
                return c3

            lax.fori_loop(0, OFF, contact, 0, unroll=4)

            def update(i, c3):
                r = ridx[i]
                own_part = dot_nt(low[i], diag[r]).reshape(6, 32, 128)
                extra = chain[last[i]].reshape(6, 32, 128)
                step = ((coupling[r] - extra) * rdiag[i][None] - own_part) * dinv[i][None]
                new = state[i] + step.reshape(192, 128)
                state[i] = new
                low[i] = new.astype(BF16)
                return c3

            lax.fori_loop(0, ROWS, update, 0, unroll=4)
            return c2

        lax.fori_loop(0, SWEEPS, sweep, 0)

        lane = iota((32, 128), 1)
        for c in range(4):
            for h in range(2):
                acc = jnp.zeros((192, 128), F32)
                for a in range(c + 1):
                    i = static_row(c, h, a)
                    x = state[i]
                    high = low[i]
                    acc = acc + dot_nt(high, weights[i])
                    acc = acc + dot_nt((x - high.astype(F32)).astype(BF16), weights[i])
                    for j in range(6):
                        stage[pl.ds(h * 32 * MSG + BASE[c] + a * 6 + j, 32, stride=MSG), :] = x[
                            j * 32 : (j + 1) * 32
                        ]
                t = acc[0:32]
                for j in range(1, 6):
                    t = t + pltpu.roll(acc[j * 32 : (j + 1) * 32], 8 * j, axis=1)
                t = t + pltpu.roll(t, 64, axis=1)
                v = vcls[c * 2 + h]
                tangent = aff[v] - t / (128.0 * (c + 1))
                row = jnp.where(lane < 48, tangent, jnp.where(lane == 64, v.astype(F32), 0.0))
                stage[pl.ds(h * 32 * MSG + 60 + c, 32, stride=MSG), :] = row

        def lower(i, c2):
            at = pl.multiple_of(i * 2 * MSG, 2 * MSG)
            back[p, pl.ds(2 * i, 2)] = (
                stage[pl.ds(at, 2 * MSG), :].astype(BF16).reshape(2, MSG, 128)
            )
            return c2

        lax.fori_loop(0, 32, lower, 0, unroll=4)

        def push_tail(step, c2):
            ty, tb, t = chip_peer(step, p, sec, bulk)
            pltpu.make_async_remote_copy(
                src_ref=back.at[p, t // 2, pl.ds(48, 16)],
                dst_ref=tails.at[me],
                send_sem=tail_send,
                recv_sem=tail_recv,
                device_id=(ty, tb),
                device_id_type=MESH,
            ).start()
            return c2

        def push_body(step, c2):
            ty, tb, t = chip_peer(step, p, sec, bulk)
            pltpu.make_async_remote_copy(
                src_ref=back.at[p, t // 2, pl.ds(0, 48)],
                dst_ref=body.at[me],
                send_sem=body_send,
                recv_sem=body_recv,
                device_id=(ty, tb),
                device_id_type=MESH,
            ).start()
            return c2

        lax.fori_loop(1, N_DEV // 2, push_tail, 0)

        @pl.when(core != p)
        def _():
            push_tail(0, 0)

        lax.fori_loop(1, N_DEV // 2, push_body, 0)

        @pl.when(core != p)
        def _():
            push_body(0, 0)

        return carry

    lax.fori_loop(0, 2, phase, 0)
    mine_back = back.at[core, me // 2]
    own_tail = pltpu.make_async_copy(mine_back.at[pl.ds(48, 16)], tails.at[me], own_sems.at[0])
    own_body = pltpu.make_async_copy(mine_back.at[pl.ds(0, 48)], body.at[me], own_sems.at[1])
    own_tail.start()
    own_body.start()

    where_to = pmap[...]
    owner = where_to // ELEM
    volume = (lax.rem(where_to, ELEM) // 64).astype(F32)
    same_owner = iota((N_DEV, ELEM), 0) == owner
    own_tail.wait()
    landed = tails.at[pl.ds(0, N_DEV - 1)]
    pltpu.make_async_copy(landed, landed, tail_recv).wait()
    wide[...] = tails[...].astype(F32).reshape(N_DEV * 16, 128)
    keep = pltpu.make_async_copy(tails, tail, own_sems.at[2])
    keep.start()
    tangent = jnp.zeros((128, ELEM), F32)
    for c in range(4):
        part = wide[pl.ds(12 + c, N_DEV, stride=16), :]
        code = jnp.broadcast_to(part[:, 64:65], (N_DEV, ELEM))
        pick = jnp.where(same_owner & (code == volume), 1.0, 0.0).astype(BF16)
        tangent = tangent + dot_nn(jnp.transpose(part).astype(BF16), pick)
    weight = volume_ref[...]
    macro_rows = [srows[i : i + 1, :] for i in range(6)]
    residual = (
        assemble(grads, conn, apply_tangent(tangent, macro_rows, weight), small_e) - load_ref[...]
    )
    residual_ref[...] = residual
    mine[...] = jnp.broadcast_to(
        jnp.sum(jnp.sum(residual * residual, axis=1, keepdims=True), axis=0, keepdims=True),
        (8, 128),
    )
    norms[me] = mine[...]

    def push_norm(step, carry):
        ty, tb, t = peer_of(step, sec, bulk)
        pltpu.make_async_remote_copy(
            src_ref=mine,
            dst_ref=norms.at[me],
            send_sem=norm_send,
            recv_sem=norm_recv,
            device_id=(ty, tb),
            device_id_type=MESH,
        ).start()
        return carry

    lax.fori_loop(1, N_DEV, push_norm, 0)
    trial = strain_rows(gather_nodes(residual, conn, small), grads)
    product_ref[...] = assemble(grads, conn, apply_tangent(tangent, trial, weight), small_e)
    arrived = norms.at[pl.ds(0, N_DEV - 1)]
    pltpu.make_async_copy(arrived, arrived, norm_recv).wait()
    total = jnp.sum(norms[...], axis=0)[0:1, :]
    root = jnp.sqrt(total / (3.0 * 16384) + 1e-06)
    update_ref[...] = -jnp.minimum(1.0, 1.0 / root) * residual

    sent = send.at[pl.ds(0, N_DEV - 1)]
    pltpu.make_async_copy(sent, sent, go_send).wait()
    pltpu.make_async_copy(arrived, arrived, norm_send).wait()
    keep.wait()
    own_body.wait()
    pltpu.make_async_copy(landed, landed, tail_send).wait()
    rest = body.at[pl.ds(0, N_DEV - 1)]
    pltpu.make_async_copy(rest, rest, body_send).wait()
    pltpu.make_async_copy(rest, rest, body_recv).wait()


def unpack_kernel(
    residual, product, update, tail, body, pmap,
    out_residual, out_product, out_update, out_hbm,
    stage, spread, rows, flat, result, sems,
):
    out_residual[...] = residual[...]
    out_product[...] = product[...]
    out_update[...] = update[...]
    make_spread(spread)

    def widen(i, carry):
        at = pl.multiple_of(i * MSG, MSG)
        stage[pl.ds(at, 48), :] = body[i].astype(F32)
        stage[pl.ds(at + 48, 16), :] = tail[i].astype(F32)
        return carry

    lax.fori_loop(0, N_DEV, widen, 0, unroll=8)
    where_to = pmap[...].astype(F32)
    column = jnp.transpose(jnp.broadcast_to(where_to, (128, ELEM))).astype(I32)
    owner = column // ELEM
    volume = lax.rem(column, ELEM) // 64
    same_owner = iota((ELEM, N_DEV), 1) == owner
    picks = []
    for c in range(4):
        part = stage[pl.ds(60 + c, N_DEV, stride=MSG), :]
        code = jnp.transpose(part)[64:65, :].astype(I32)
        picks.append(jnp.where(same_owner & (code == volume), 1.0, 0.0).astype(BF16))
    pick = jnp.concatenate(picks, axis=1)
    copies = []
    for a in range(4):
        for c in range(a, 4):
            for j in range(6):
                rows[c * 128 : (c + 1) * 128, j * 128 : (j + 1) * 128] = stage[
                    pl.ds(BASE[c] + a * 6 + j, N_DEV, stride=MSG), :
                ].astype(BF16)
        flat[a * 128 :, :] = dot_nt(rows[a * 128 :, :], spread[...]).astype(BF16)
        result[:, a * LEVEL : (a + 1) * LEVEL] = dot_nn(
            pick[:, a * 128 :], flat[a * 128 :, :]
        ).astype(BF16)
        part = pl.ds(a * LEVEL, LEVEL)
        copy = pltpu.make_async_copy(result.at[:, part], out_hbm.at[:, part], sems.at[a])
        copy.start()
        copies.append(copy)
    for copy in copies:
        copy.wait()


def forces_of(grads_ref, s):
    g = [[grads_ref[3 * a + k : 3 * a + k + 1, :] for k in range(3)] for a in range(4)]
    out = []
    for a in range(4):
        gx, gy, gz = g[a]
        out.append(
            (
                gx * s[0] + gz * s[4] + gy * s[5],
                gy * s[1] + gz * s[3] + gx * s[5],
                gz * s[2] + gy * s[3] + gx * s[4],
            )
        )
    return out


def assemble(grads_ref, conn_ref, stress, scratch):
    forces = forces_of(grads_ref, stress)
    total = jnp.zeros((8, NODE), F32)
    for a in range(4):
        scratch[...] = jnp.zeros_like(scratch)
        for k in range(3):
            f = forces[a][k]
            high = f.astype(BF16).astype(F32)
            rest = f - high
            middle = rest.astype(BF16).astype(F32)
            scratch[k : k + 1, :] = high
            scratch[8 + k : 9 + k, :] = middle
            scratch[16 + k : 17 + k, :] = rest - middle
        part = dot_nt(scratch[...].astype(BF16), node_onehot(conn_ref, a))
        total = total + (part[0:8] + part[8:16] + part[16:24])
    return total[0:3]


def apply_tangent(tangent, strain, weight):
    acc = tangent[0:8] * strain[0]
    for j in range(1, 6):
        acc = acc + tangent[8 * j : 8 * j + 8] * strain[j]
    acc = acc * weight
    return [acc[i : i + 1, :] for i in range(6)]


VMEM = pl.BlockSpec(memory_space=pltpu.VMEM)
SMEM = pl.BlockSpec(memory_space=pltpu.SMEM)
ANY = pl.BlockSpec(memory_space=pl.ANY)
DMA = pltpu.SemaphoreType.DMA


def params(collective_id=None, limit=48):
    return pltpu.CompilerParams(
        collective_id=collective_id,
        has_side_effects=collective_id is not None,
        vmem_limit_bytes=limit * 2**20,
    )


def on_device(
    displacement, nodal_load, connectivity, shape_grads, elem_volume, point_map, vol_blocks,
    c_affine, coupling, diag_blocks, diag_normal, off_blocks, off_row, off_col, off_normal,
    off_count, fluct_state,
):
    pmap = point_map.reshape(1, ELEM)
    volume = elem_volume.reshape(1, ELEM)
    smem = lambda n: pltpu.SMEM((n,), I32)
    vmem = pltpu.VMEM
    nodal = jax.ShapeDtypeStruct((3, NODE), F32)
    tail, body, residual, product, update = pl.pallas_call(
        step_kernel,
        out_shape=(
            jax.ShapeDtypeStruct((N_DEV, 16, 128), BF16),
            jax.ShapeDtypeStruct((N_DEV, 48, 128), BF16),
            nodal, nodal, nodal,
        ),
        in_specs=[VMEM] * 6 + [SMEM, VMEM] + [SMEM] * 5 + [ANY] * 4,
        out_specs=(ANY, ANY, VMEM, VMEM, VMEM),
        scratch_shapes=[
            vmem((ELEM, 4 * LEVEL), BF16),
            vmem((N_DEV * MSG, 128), F32),
            vmem((N_DEV, MSG, 128), BF16),
            vmem((LEVEL, LEVEL), BF16),
            vmem((1280, LEVEL), BF16),
            vmem((128, ELEM), F32),
            vmem((32, 128), F32),
            vmem((32, ELEM), F32),
            vmem((2, 64, MSG, 128), BF16),
            vmem((2, 64, MSG, 128), BF16),
            vmem((ROWS, 6, 1, 128), F32),
            vmem((ROWS, 128, 128), BF16),
            vmem((OFF, 128, 128), BF16),
            vmem((ROWS, 192, 128), F32),
            vmem((ROWS, 192, 128), BF16),
            vmem((OFF + 1, 192, 128), F32),
            vmem((32, 32, 128), F32),
            vmem((48, 32, 128), F32),
            vmem((ROWS, 32, 128), F32),
            vmem((OFF, 32, 128), F32),
            vmem((ROWS, 1, 128), F32),
            vmem((ROWS, 128, 128), BF16),
            vmem((8, 1, 128), F32),
            vmem((N_DEV, 16, 128), BF16),
            vmem((N_DEV * 16, 128), F32),
            vmem((8, 128), F32),
            vmem((N_DEV, 8, 128), F32),
            smem(8), smem(ROWS), smem(ROWS), smem(ROWS), smem(ROWS),
            smem(OFF), smem(OFF), smem(OFF), smem(OFF),
            DMA((4,)), DMA((3,)), DMA, DMA((2,)), DMA, DMA, DMA, DMA, DMA, DMA,
        ],
        compiler_params=params(1, 60),
        name="step",
    )(
        displacement, nodal_load, connectivity, shape_grads, volume, pmap, vol_blocks, c_affine,
        diag_normal.transpose(2, 1, 0), off_normal.transpose(2, 1, 0), off_row.T, off_col.T,
        off_count, coupling.transpose(0, 2, 1, 3), diag_blocks[:, 0], off_blocks[:, 0],
        fluct_state,
    )
    return pl.pallas_call(
        unpack_kernel,
        out_shape=(nodal, nodal, nodal, jax.ShapeDtypeStruct((ELEM, 4 * LEVEL), BF16)),
        in_specs=[VMEM] * 6,
        out_specs=(VMEM, VMEM, VMEM, ANY),
        scratch_shapes=[
            vmem((N_DEV * MSG, 128), F32),
            vmem((LEVEL, LEVEL), BF16),
            vmem((512, LEVEL), BF16),
            vmem((512, LEVEL), BF16),
            vmem((ELEM, 4 * LEVEL), BF16),
            DMA((4,)),
        ],
        compiler_params=params(None, 60),
        name="unpack",
    )(residual, product, update, tail, body, pmap)


def solution(mesh):
    both = ("sec", "bulk")
    return jax.shard_map(
        on_device,
        mesh=mesh,
        in_specs=(
            P(None, both), P(None, both), P(None, both), P(None, both), P(both), P(both),
            P("bulk", None), P("bulk", None, None), P(None, "bulk", None, None),
            P(None, "bulk", None, None), P(None, "bulk", None), P(None, "bulk", None, None),
            P(None, "bulk"), P(None, "bulk"), P(None, "bulk", None), P("bulk"), P(both, None),
        ),
        out_specs=(P(None, both), P(None, both), P(None, both), P(both, None)),
        check_vma=False,
    )
```

```python
import jax
import jax.numpy as jnp
from jax import lax
from jax.experimental import pallas as pl
from jax.experimental.pallas import tpu as pltpu
from jax.sharding import PartitionSpec as P

F32 = jnp.float32
BF16 = jnp.bfloat16
I32 = jnp.int32
N_DEV = 128
ELEM = 512
NODE = 128
LEVEL = 768
MSG = 64
SWEEPS = 3
ROWS = 20
OFF = 32
MESH = pl.DeviceIdType.MESH
BASE = (0, 6, 18, 36)
SLOT0 = (0, 2, 6, 12)
SKEW_Y = 2
SKEW_Z = 3
EARLY = 14


def dot_nt(a, b):
    return lax.dot_general(a, b, (((1,), (1,)), ((), ())), preferred_element_type=F32)


def dot_nn(a, b):
    return lax.dot_general(a, b, (((1,), (0,)), ((), ())), preferred_element_type=F32)


def iota(shape, dim):
    return lax.broadcasted_iota(I32, shape, dim)


def static_row(c, h, a):
    return SLOT0[c] + h * (c + 1) + a


def my_position():
    sec = lax.axis_index("sec")
    bulk = lax.axis_index("bulk")
    return sec, bulk, sec * 32 + bulk


def wrap(x):
    return x - jnp.where(x >= 4, 4, 0)


def each_peer(sec, bulk, act, core=None):
    bx, bz, bc = bulk // 8, lax.rem(bulk // 2, 4), lax.rem(bulk, 2)
    columns = [wrap(bx + dx) * 8 for dx in range(4)]
    cores = [bc, 1 - bc] if core is None else [core]

    def block(step, first):
        ty0, tz0 = wrap(sec + step // 4), wrap(bz + lax.rem(step, 4))
        for m in range(first, 4 * len(cores)):
            dx = m % 4
            ty = wrap(ty0 + (SKEW_Y * dx) % 4)
            tb = columns[dx] + wrap(tz0 + (SKEW_Z * dx) % 4) * 2 + cores[m // 4]
            act(step, ty, tb, ty * 32 + tb)

    block(jnp.int32(0), 1)

    def body(step, carry):
        block(step, 0)
        return carry

    lax.fori_loop(1, 16, body, 0)


def greet_all(barrier, sec, bulk):
    def greet(step, ty, tb, t):
        pl.semaphore_signal(barrier, inc=1, device_id=(ty, tb), device_id_type=MESH)

    each_peer(sec, bulk, greet)


def split3(nodal, scratch):
    high = nodal.astype(BF16).astype(F32)
    rest = nodal - high
    middle = rest.astype(BF16).astype(F32)
    low = rest - middle
    scratch[...] = jnp.zeros_like(scratch)
    rows = nodal.shape[0]
    scratch[0:rows, :] = high
    scratch[8 : 8 + rows, :] = middle
    scratch[16 : 16 + rows, :] = low
    return scratch[...].astype(BF16)


def node_onehot(conn_ref, a):
    ids = conn_ref[a : a + 1, :]
    return jnp.where(iota((NODE, ELEM), 0) == ids, 1.0, 0.0).astype(BF16)


def gather_nodes(nodal, conn_ref, scratch):
    parts = split3(nodal, scratch)
    out = []
    for a in range(4):
        got = dot_nn(parts, node_onehot(conn_ref, a))
        out.append(got[0:8] + got[8:16] + got[16:24])
    return out


def strain_rows(moved, grads_ref):
    g = [[grads_ref[3 * a + k : 3 * a + k + 1, :] for k in range(3)] for a in range(4)]
    u = [[moved[a][k : k + 1, :] for k in range(3)] for a in range(4)]

    def total(terms):
        out = terms[0]
        for t in terms[1:]:
            out = out + t
        return out

    return [
        total([g[a][0] * u[a][0] for a in range(4)]),
        total([g[a][1] * u[a][1] for a in range(4)]),
        total([g[a][2] * u[a][2] for a in range(4)]),
        total([g[a][2] * u[a][1] + g[a][1] * u[a][2] for a in range(4)]),
        total([g[a][2] * u[a][0] + g[a][0] * u[a][2] for a in range(4)]),
        total([g[a][1] * u[a][0] + g[a][0] * u[a][1] for a in range(4)]),
    ]


def make_spread(spread):
    n = iota((1, LEVEL), 1)
    source = lax.rem(n, 128) * 6 + n // 128
    spread[...] = jnp.where(iota((LEVEL, LEVEL), 0) == source, 1.0, 0.0).astype(BF16)


def to_rows(rows):
    n = iota((1, 8 * rows), 1)
    target = lax.rem(n, rows) * 8 + n // rows
    return jnp.where(iota((8 * rows, 8 * rows), 0) == target, 1.0, 0.0).astype(BF16)


def to_slots(rows):
    n = iota((1, 8 * rows), 1)
    target = lax.rem(n, 8) * rows + n // 8
    return jnp.where(iota((8 * rows, 8 * rows), 0) == target, 1.0, 0.0).astype(BF16)


def two_rows(first, second):
    return jnp.concatenate([first, second], axis=0).astype(BF16)


def side_by_side(ref, at, rows):
    parts = [ref[pl.ds(at + 8 * i, 8)].reshape(8 * rows, 128) for i in range(2)]
    return jnp.concatenate(parts, axis=1)


def prepare_send(strain, pmap, state, ends, mixed, slots, send, spread, flat, srows, load):
    srows[...] = jnp.zeros_like(srows)
    for i in range(6):
        srows[i : i + 1, :] = strain[i]
    where_to = pmap[...]
    owner = where_to // ELEM
    volume = lax.rem(where_to, ELEM) // 64
    srows[8:9, :] = volume.astype(F32)
    strain_low = srows[...].astype(BF16)
    make_spread(spread)
    load.wait()

    ones = jnp.ones((16, LEVEL), BF16)
    levels = jnp.zeros((1, ELEM), I32)
    for a in range(4):
        weight = dot_nt(ones, jnp.abs(state[:, a * LEVEL : (a + 1) * LEVEL]))[0:1, :]
        levels = jnp.where(weight > 0.0, a + 1, levels)
    key = (owner * 4096 + levels * 512 + iota((1, ELEM), 1)).astype(F32)
    key_col = jnp.transpose(jnp.broadcast_to(key, (128, ELEM)))
    order = []
    for m in range(4):
        part = key[:, m * 128 : (m + 1) * 128]
        order.append(jnp.sum(jnp.where(key_col < part, 1.0, 0.0), axis=0, keepdims=True))
    order = jnp.concatenate(order, axis=1).astype(I32)

    at = 0
    for k in range(4):
        pick = jnp.where(order == iota((N_DEV, ELEM), 0) * 4 + k, 1.0, 0.0).astype(BF16)
        for a in range(k + 1):
            mine = dot_nn(pick, state[:, a * LEVEL : (a + 1) * LEVEL])
            flat[at * 128 : (at + 1) * 128, :] = mine.astype(BF16)
            at += 1
        ends[k] = dot_nt(pick, strain_low)
    for jj in range(3):
        for half in range(2):
            got = dot_nn(
                flat[half * 640 : (half + 1) * 640, :], spread[:, jj * 256 : (jj + 1) * 256]
            )
            for i in range(5):
                row = (half * 5 + i) * 6 + jj * 2
                for ob in range(16):
                    part = got[i * 128 + ob * 8 : i * 128 + ob * 8 + 8]
                    lane = (ob % 2) * 128
                    mixed[ob // 2, row * 8 : row * 8 + 16, lane : lane + 128] = two_rows(
                        part[:, :128], part[:, 128:]
                    )
    for k in (0, 2):
        for ob in range(16):
            lane = (ob % 2) * 128
            at = (60 + k) * 8
            mixed[ob // 2, at : at + 16, lane : lane + 128] = two_rows(
                ends[k, ob * 8 : ob * 8 + 8], ends[k + 1, ob * 8 : ob * 8 + 8]
            )
    slots[...] = to_slots(MSG)

    def lower(g, carry):
        for m in range(2):
            got = dot_nn(slots[m * 256 : (m + 1) * 256, :], mixed[g]).astype(BF16)
            for i in range(2):
                send[pl.ds(16 * g + 8 * i + 4 * m, 4)] = got[
                    :, i * 128 : (i + 1) * 128
                ].reshape(4, MSG, 128)
        return carry

    lax.fori_loop(0, 8, lower, 0)


def make_tables(vols, off_row, off_col, vcls, chrow, ridx, inv, last, prev, crow, ccol, cvol):
    sizes = [vols[0, v] for v in range(8)]
    zero = jnp.int32(0)
    halves, starts, start = [], [], zero
    for v in range(8):
        half = zero
        for w in range(v):
            half = half + jnp.where(sizes[w] == sizes[v], 1, 0)
        halves.append(half)
        starts.append(start)
        start = start + sizes[v]
    for c in range(4):
        for h in range(2):
            vol, first = zero, zero
            for v in range(8):
                hit = (sizes[v] == c + 1) & (halves[v] == h)
                vol = jnp.where(hit, v, vol)
                first = jnp.where(hit, starts[v], first)
            vcls[c * 2 + h] = vol
            for a in range(c + 1):
                ridx[static_row(c, h, a)] = first + a
                chrow[static_row(c, h, a)] = c * 2 + h

    def invert(r, carry):
        found = jnp.int32(0)
        for i in range(ROWS):
            found = jnp.where(ridx[i] == r, i, found)
        inv[r] = found
        return carry

    lax.fori_loop(0, ROWS, invert, 0)

    def ends(c, carry):
        row = inv[off_row[0, c]]
        crow[c] = row
        ccol[c] = inv[off_col[0, c]]
        cvol[c] = chrow[row]
        return carry

    lax.fori_loop(0, OFF, ends, 0)

    def link(c, carry):
        row = crow[c]
        before = jnp.int32(0)
        for k in range(OFF):
            before = jnp.where((crow[k] == row) & (k < c), k + 1, before)
        prev[c] = before
        return carry

    lax.fori_loop(0, OFF, link, 0)

    def finish(i, carry):
        end = jnp.int32(0)
        for k in range(OFF):
            end = jnp.where(crow[k] == i, k + 1, end)
        last[i] = end
        return carry

    lax.fori_loop(0, ROWS, finish, 0)


def step_kernel(
    disp, load_ref, conn, grads, volume_ref, pmap, vols, affine, diag_n, off_n, off_row,
    off_col, off_count, coupling_hbm, diag_hbm, off_hbm, state_hbm,
    tail, body, residual_ref, product_ref, update_ref,
    fluct, ends, mixed, slots, rows_of, turned, send, spread, flat, srows, small, small_e,
    got, back, coupling, diag, off,
    state, low, chain, mask, strain, rdiag, cscale, dinv, weights, aff,
    tails, parts, mine, norms,
    vcls, chrow, ridx, inv, last, prev, crow, ccol, cvol,
    load_sems, own_sems, go_send, go_recv, tail_send, tail_recv, body_send, body_recv,
    norm_send, norm_recv,
):
    sec, bulk, me = my_position()
    core = lax.rem(bulk, 2)
    barrier = pltpu.get_barrier_semaphore()
    loads = []
    for i, (source, target) in enumerate(
        [(state_hbm, fluct), (off_hbm, off), (diag_hbm, diag), (coupling_hbm, coupling)]
    ):
        loads.append(pltpu.make_async_copy(source, target, load_sems.at[i]))
        loads[-1].start()
    greet_all(barrier, sec, bulk)
    macro = strain_rows(gather_nodes(disp[...], conn, small), grads)
    prepare_send(macro, pmap, fluct, ends, mixed, slots, send, spread, flat, srows, loads[0])
    own = pltpu.make_async_copy(send.at[me], got.at[core, me // 2], own_sems.at[0])
    own.start()
    pl.semaphore_wait(barrier, N_DEV - 1)

    def push(step, ty, tb, t):
        late = jnp.where(step >= EARLY, 1, 0)
        pltpu.make_async_remote_copy(
            src_ref=send.at[t],
            dst_ref=got.at[core, me // 2],
            send_sem=go_send,
            recv_sem=go_recv.at[core, late],
            device_id=(ty, tb),
            device_id_type=MESH,
        ).start()

    @pl.when(core == 0)
    def _():
        each_peer(sec, bulk, push)

    make_tables(vols, off_row, off_col, vcls, chrow, ridx, inv, last, prev, crow, ccol, cvol)
    lanes6 = iota((36, 128), 1)
    rows6 = iota((36, 128), 0)
    place = jnp.where(lanes6 == lax.rem(rows6, 6) * 8 + rows6 // 6, 1.0, 0.0).astype(F32)
    spread_affine = lax.dot_general(
        affine[0], place, (((1,), (0,)), ((), ())),
        preferred_element_type=F32, precision=lax.Precision.HIGHEST,
    )
    for v in range(8):
        aff[v] = spread_affine[v : v + 1, :]
    eye = iota((128, 128), 0) == iota((128, 128), 1)
    for load in loads[1:]:
        load.wait()

    def prepare(i, carry):
        r = ridx[i]
        values = jnp.where(eye, diag[r].astype(F32), 0.0)
        dinv[i] = 1.0 / jnp.sum(values, axis=0, keepdims=True)
        load = coupling[r].reshape(6, 128)
        high = load.astype(BF16).astype(F32)
        block = jnp.zeros((58, 128), F32)
        weights[i] = jnp.concatenate([high, block, load - high, block], axis=0).astype(BF16)
        return carry

    lax.fori_loop(0, ROWS, prepare, 0, unroll=2)
    rows_of[...] = to_rows(MSG)
    chain[0] = jnp.zeros((192, 128), F32)
    live = off_count[0]
    own.wait()

    def phase(p, carry):
        early = 4 * EARLY

        @pl.when(core == p)
        def _():
            part = got.at[p, pl.ds(0, early - 1)]
            pltpu.make_async_copy(part, part, go_recv.at[p, 0]).wait()

        @pl.when(core != p)
        def _():
            part = got.at[p, pl.ds(0, early)]
            pltpu.make_async_copy(part, part, go_recv.at[p, 0]).wait()

        @pl.when((p == 0) & (core == 1))
        def _():
            each_peer(sec, bulk, push)

        part = got.at[p, pl.ds(0, 64 - early)]
        pltpu.make_async_copy(part, part, go_recv.at[p, 1]).wait()

        def take(g, c2):
            h = g // 2
            q0 = pl.multiple_of(lax.rem(g, 2) * 16, 16)
            turned[...] = dot_nn(rows_of[...], side_by_side(got.at[p], 16 * g, MSG))

            def message_row(r):
                part = turned[r * 8 : r * 8 + 8, :]
                return jnp.concatenate([part[:, :128], part[:, 128:]], axis=0)

            rest = [message_row(60 + k) for k in range(4)]
            for c in range(4):
                v = vcls[c * 2 + h].astype(F32)
                picked = jnp.zeros((16, 128), F32)
                for k in range(4):
                    code = jnp.broadcast_to(rest[k][:, 8:9], (16, 128))
                    m = jnp.where(code == v, 1.0, 0.0)
                    mask[c * 4 + k] = m
                    picked = picked + m * rest[k]
                for i in range(6):
                    strain[(c * 2 + h) * 6 + i, pl.ds(q0, 16), :] = jnp.broadcast_to(
                        picked[:, i : i + 1], (16, 128)
                    )
            for a in range(4):
                for j in range(6):
                    sums = {}
                    for k in range(a, 4):
                        part = message_row(BASE[k] + a * 6 + j)
                        for c in range(a, 4):
                            term = mask[c * 4 + k] * part
                            sums[c] = sums[c] + term if c in sums else term
                    for c in range(a, 4):
                        i = static_row(c, h, a)
                        at = pl.multiple_of(j * 32 + q0, 16)
                        state[i, pl.ds(at, 16), :] = sums[c]
                        low[i, pl.ds(at, 16), :] = sums[c].astype(BF16)
            return c2

        lax.fori_loop(0, 4, take, 0)

        def row_scale(i, c2):
            r = ridx[i]
            ch = chrow[i] * 6
            z = diag_n[0, 0, r] * strain[ch]
            for k in range(1, 6):
                z = z + diag_n[k, 0, r] * strain[ch + k]
            rdiag[i] = 1.0 / (1.0 + 0.4 * jnp.tanh(z))
            return c2

        lax.fori_loop(0, ROWS, row_scale, 0, unroll=5)

        def contact_scale(c, c2):
            ch = cvol[c] * 6
            z = off_n[0, 0, c] * strain[ch]
            for k in range(1, 6):
                z = z + off_n[k, 0, c] * strain[ch + k]
            on = jnp.where(c < live, 1.0, 0.0).astype(F32)
            cscale[c] = (1.0 + 0.4 * jnp.tanh(z)) * on
            return c2

        lax.fori_loop(0, OFF, contact_scale, 0, unroll=8)

        def sweep(n, c2):
            def contact(c, c3):
                value = dot_nt(low[ccol[c]], off[c]).reshape(6, 32, 128)
                scaled = (value * cscale[c][None]).reshape(192, 128)
                chain[c + 1] = chain[prev[c]] + scaled
                return c3

            lax.fori_loop(0, OFF, contact, 0, unroll=16)

            def update(i, c3):
                r = ridx[i]
                own_part = dot_nt(low[i], diag[r]).reshape(6, 32, 128)
                extra = chain[last[i]].reshape(6, 32, 128)
                step = ((coupling[r] - extra) * rdiag[i][None] - own_part) * dinv[i][None]
                new = state[i] + step.reshape(192, 128)
                state[i] = new
                low[i] = new.astype(BF16)
                return c3

            lax.fori_loop(0, ROWS, update, 0, unroll=10)
            return c2

        lax.fori_loop(0, SWEEPS, sweep, 0)

        lane = iota((32, 128), 1)
        for h in range(2):
            last_rows = []
            for c in range(4):
                acc = jnp.zeros((192, 128), F32)
                for a in range(c + 1):
                    i = static_row(c, h, a)
                    x = state[i]
                    high = low[i]
                    acc = acc + dot_nt(high, weights[i])
                    acc = acc + dot_nt((x - high.astype(F32)).astype(BF16), weights[i])
                    for j in range(0, 6, 2):
                        at = (BASE[c] + a * 6 + j) * 8
                        for q in range(4):
                            cols = (q % 2) * 128
                            mixed[h * 2 + q // 2, at : at + 16, cols : cols + 128] = two_rows(
                                x[j * 32 + q * 8 : j * 32 + q * 8 + 8],
                                x[j * 32 + 32 + q * 8 : j * 32 + 40 + q * 8],
                            )
                t = acc[0:32]
                for j in range(1, 6):
                    t = t + pltpu.roll(acc[j * 32 : (j + 1) * 32], 8 * j, axis=1)
                t = t + pltpu.roll(t, 64, axis=1)
                v = vcls[c * 2 + h]
                tangent = aff[v] - t / (128.0 * (c + 1))
                last_rows.append(
                    jnp.where(lane < 48, tangent, jnp.where(lane == 64, v.astype(F32), 0.0))
                )
            for k in (0, 2):
                at = (60 + k) * 8
                for q in range(4):
                    cols = (q % 2) * 128
                    mixed[h * 2 + q // 2, at : at + 16, cols : cols + 128] = two_rows(
                        last_rows[k][q * 8 : q * 8 + 8], last_rows[k + 1][q * 8 : q * 8 + 8]
                    )

        def lower(g, c2):
            for m in range(2):
                out = dot_nn(slots[m * 256 : (m + 1) * 256, :], mixed[g]).astype(BF16)
                for i in range(2):
                    back[p, pl.ds(16 * g + 8 * i + 4 * m, 4)] = out[
                        :, i * 128 : (i + 1) * 128
                    ].reshape(4, MSG, 128)
            return c2

        lax.fori_loop(0, 4, lower, 0)

        def push_tail(step, ty, tb, t):
            pltpu.make_async_remote_copy(
                src_ref=back.at[p, t // 2, pl.ds(48, 16)],
                dst_ref=tails.at[me],
                send_sem=tail_send,
                recv_sem=tail_recv,
                device_id=(ty, tb),
                device_id_type=MESH,
            ).start()

        def push_body(step, ty, tb, t):
            pltpu.make_async_remote_copy(
                src_ref=back.at[p, t // 2, pl.ds(0, 48)],
                dst_ref=body.at[me],
                send_sem=body_send,
                recv_sem=body_recv,
                device_id=(ty, tb),
                device_id_type=MESH,
            ).start()

        partner = bulk + 1 - 2 * core
        for push_part in (push_tail, push_body):
            each_peer(sec, bulk, push_part, p)

            @pl.when(core != p)
            def _():
                push_part(0, sec, partner, sec * 32 + partner)

        return carry

    lax.fori_loop(0, 2, phase, 0)
    mine_back = back.at[core, me // 2]
    own_tail = pltpu.make_async_copy(mine_back.at[pl.ds(48, 16)], tails.at[me], own_sems.at[0])
    own_body = pltpu.make_async_copy(mine_back.at[pl.ds(0, 48)], body.at[me], own_sems.at[1])
    own_tail.start()
    own_body.start()

    where_to = pmap[...]
    owner = where_to // ELEM
    volume = (lax.rem(where_to, ELEM) // 64).astype(F32)
    same_owner = iota((N_DEV, ELEM), 0) == owner
    own_tail.wait()
    landed = tails.at[pl.ds(0, N_DEV - 1)]
    pltpu.make_async_copy(landed, landed, tail_recv).wait()
    keep = pltpu.make_async_copy(tails, tail, own_sems.at[2])
    keep.start()
    turn = to_rows(16)[96:128]
    for g in range(8):
        out = dot_nn(turn, side_by_side(tails, 16 * g, 16))
        for c in range(4):
            for i in range(2):
                parts[c, 16 * g + 8 * i : 16 * g + 8 * i + 8, :] = out[
                    c * 8 : c * 8 + 8, i * 128 : (i + 1) * 128
                ]
    tangent = jnp.zeros((128, ELEM), F32)
    for c in range(4):
        part = parts[c]
        code = jnp.broadcast_to(part[:, 64:65], (N_DEV, ELEM))
        pick = jnp.where(same_owner & (code == volume), 1.0, 0.0).astype(BF16)
        tangent = tangent + dot_nn(jnp.transpose(part).astype(BF16), pick)
    weight = volume_ref[...]
    macro_rows = [srows[i : i + 1, :] for i in range(6)]
    residual = (
        assemble(grads, conn, apply_tangent(tangent, macro_rows, weight), small_e) - load_ref[...]
    )
    residual_ref[...] = residual
    mine[...] = jnp.broadcast_to(
        jnp.sum(jnp.sum(residual * residual, axis=1, keepdims=True), axis=0, keepdims=True),
        (8, 128),
    )
    norms[me] = mine[...]

    def push_norm(step, ty, tb, t):
        pltpu.make_async_remote_copy(
            src_ref=mine,
            dst_ref=norms.at[me],
            send_sem=norm_send,
            recv_sem=norm_recv,
            device_id=(ty, tb),
            device_id_type=MESH,
        ).start()

    each_peer(sec, bulk, push_norm)
    trial = strain_rows(gather_nodes(residual, conn, small), grads)
    product_ref[...] = assemble(grads, conn, apply_tangent(tangent, trial, weight), small_e)
    arrived = norms.at[pl.ds(0, N_DEV - 1)]
    pltpu.make_async_copy(arrived, arrived, norm_recv).wait()
    total = jnp.sum(norms[...], axis=0)[0:1, :]
    root = jnp.sqrt(total / (3.0 * 16384) + 1e-06)
    update_ref[...] = -jnp.minimum(1.0, 1.0 / root) * residual

    sent = send.at[pl.ds(0, N_DEV - 1)]
    pltpu.make_async_copy(sent, sent, go_send).wait()
    pltpu.make_async_copy(arrived, arrived, norm_send).wait()
    keep.wait()
    own_body.wait()
    pltpu.make_async_copy(landed, landed, tail_send).wait()
    rest = body.at[pl.ds(0, N_DEV - 1)]
    pltpu.make_async_copy(rest, rest, body_send).wait()
    pltpu.make_async_copy(rest, rest, body_recv).wait()


def unpack_kernel(
    residual, product, update, tail, body, pmap,
    out_residual, out_product, out_update, out_hbm,
    parts, spread, rows, flat, result, sems,
):
    out_residual[...] = residual[...]
    out_product[...] = product[...]
    out_update[...] = update[...]
    make_spread(spread)

    turn_body = to_rows(48)
    turn_tail = to_rows(16)
    for g in range(8):
        main = dot_nn(turn_body, side_by_side(body, 16 * g, 48))
        end = dot_nn(turn_tail, side_by_side(tail, 16 * g, 16))
        for r in range(60):
            source, at = (main, r) if r < 48 else (end, r - 48)
            part = source[at * 8 : at * 8 + 8]
            rows[r // 6, 16 * g : 16 * g + 16, (r % 6) * 128 : (r % 6 + 1) * 128] = two_rows(
                part[:, :128], part[:, 128:]
            )
        for c in range(4):
            part = end[(12 + c) * 8 : (12 + c) * 8 + 8]
            for i in range(2):
                parts[c, 16 * g + 8 * i : 16 * g + 8 * i + 8, :] = part[
                    :, i * 128 : (i + 1) * 128
                ]
    where_to = pmap[...].astype(F32)
    column = jnp.transpose(jnp.broadcast_to(where_to, (128, ELEM))).astype(I32)
    owner = column // ELEM
    volume = lax.rem(column, ELEM) // 64
    same_owner = iota((ELEM, N_DEV), 1) == owner
    picks = []
    for c in range(4):
        code = jnp.transpose(parts[c])[64:65, :].astype(I32)
        picks.append(jnp.where(same_owner & (code == volume), 1.0, 0.0).astype(BF16))
    pick = jnp.concatenate(picks, axis=1)
    copies = []
    for a in range(4):
        for c in range(a, 4):
            level = rows[BASE[c] // 6 + a]
            flat[c * 128 : (c + 1) * 128, :] = dot_nt(level, spread[...]).astype(BF16)
        result[:, a * LEVEL : (a + 1) * LEVEL] = dot_nn(
            pick[:, a * 128 :], flat[a * 128 :, :]
        ).astype(BF16)
        part = pl.ds(a * LEVEL, LEVEL)
        copy = pltpu.make_async_copy(result.at[:, part], out_hbm.at[:, part], sems.at[a])
        copy.start()
        copies.append(copy)
    for copy in copies:
        copy.wait()


def forces_of(grads_ref, s):
    g = [[grads_ref[3 * a + k : 3 * a + k + 1, :] for k in range(3)] for a in range(4)]
    out = []
    for a in range(4):
        gx, gy, gz = g[a]
        out.append(
            (
                gx * s[0] + gz * s[4] + gy * s[5],
                gy * s[1] + gz * s[3] + gx * s[5],
                gz * s[2] + gy * s[3] + gx * s[4],
            )
        )
    return out


def assemble(grads_ref, conn_ref, stress, scratch):
    forces = forces_of(grads_ref, stress)
    total = jnp.zeros((8, NODE), F32)
    for a in range(4):
        scratch[...] = jnp.zeros_like(scratch)
        for k in range(3):
            f = forces[a][k]
            high = f.astype(BF16).astype(F32)
            rest = f - high
            middle = rest.astype(BF16).astype(F32)
            scratch[k : k + 1, :] = high
            scratch[8 + k : 9 + k, :] = middle
            scratch[16 + k : 17 + k, :] = rest - middle
        part = dot_nt(scratch[...].astype(BF16), node_onehot(conn_ref, a))
        total = total + (part[0:8] + part[8:16] + part[16:24])
    return total[0:3]


def apply_tangent(tangent, strain, weight):
    acc = tangent[0:8] * strain[0]
    for j in range(1, 6):
        acc = acc + tangent[8 * j : 8 * j + 8] * strain[j]
    acc = acc * weight
    return [acc[i : i + 1, :] for i in range(6)]


VMEM = pl.BlockSpec(memory_space=pltpu.VMEM)
SMEM = pl.BlockSpec(memory_space=pltpu.SMEM)
ANY = pl.BlockSpec(memory_space=pl.ANY)
DMA = pltpu.SemaphoreType.DMA


def params(collective_id=None, limit=48):
    return pltpu.CompilerParams(
        collective_id=collective_id,
        has_side_effects=collective_id is not None,
        vmem_limit_bytes=limit * 2**20,
    )


def on_device(
    displacement, nodal_load, connectivity, shape_grads, elem_volume, point_map, vol_blocks,
    c_affine, coupling, diag_blocks, diag_normal, off_blocks, off_row, off_col, off_normal,
    off_count, fluct_state,
):
    pmap = point_map.reshape(1, ELEM)
    volume = elem_volume.reshape(1, ELEM)
    smem = lambda n: pltpu.SMEM((n,), I32)
    vmem = pltpu.VMEM
    nodal = jax.ShapeDtypeStruct((3, NODE), F32)
    tail, body, residual, product, update = pl.pallas_call(
        step_kernel,
        out_shape=(
            jax.ShapeDtypeStruct((N_DEV, 16, 128), BF16),
            jax.ShapeDtypeStruct((N_DEV, 48, 128), BF16),
            nodal, nodal, nodal,
        ),
        in_specs=[VMEM] * 6 + [SMEM, VMEM] + [SMEM] * 5 + [ANY] * 4,
        out_specs=(ANY, ANY, VMEM, VMEM, VMEM),
        scratch_shapes=[
            vmem((ELEM, 4 * LEVEL), BF16),
            vmem((4, N_DEV, 128), F32),
            vmem((8, 512, 256), BF16),
            vmem((512, 512), BF16),
            vmem((512, 512), BF16),
            vmem((512, 256), F32),
            vmem((N_DEV, MSG, 128), BF16),
            vmem((LEVEL, LEVEL), BF16),
            vmem((1280, LEVEL), BF16),
            vmem((128, ELEM), F32),
            vmem((32, 128), F32),
            vmem((32, ELEM), F32),
            vmem((2, 64, MSG, 128), BF16),
            vmem((2, 64, MSG, 128), BF16),
            vmem((ROWS, 6, 1, 128), F32),
            vmem((ROWS, 128, 128), BF16),
            vmem((OFF, 128, 128), BF16),
            vmem((ROWS, 192, 128), F32),
            vmem((ROWS, 192, 128), BF16),
            vmem((OFF + 1, 192, 128), F32),
            vmem((16, 16, 128), F32),
            vmem((48, 32, 128), F32),
            vmem((ROWS, 32, 128), F32),
            vmem((OFF, 32, 128), F32),
            vmem((ROWS, 1, 128), F32),
            vmem((ROWS, 128, 128), BF16),
            vmem((8, 1, 128), F32),
            vmem((N_DEV, 16, 128), BF16),
            vmem((4, N_DEV, 128), F32),
            vmem((8, 128), F32),
            vmem((N_DEV, 8, 128), F32),
            smem(8), smem(ROWS), smem(ROWS), smem(ROWS), smem(ROWS),
            smem(OFF), smem(OFF), smem(OFF), smem(OFF),
            DMA((4,)), DMA((3,)), DMA, DMA((2, 2)), DMA, DMA, DMA, DMA, DMA, DMA,
        ],
        compiler_params=params(1, 60),
        name="step",
    )(
        displacement, nodal_load, connectivity, shape_grads, volume, pmap, vol_blocks, c_affine,
        diag_normal.transpose(2, 1, 0), off_normal.transpose(2, 1, 0), off_row.T, off_col.T,
        off_count, coupling.transpose(0, 2, 1, 3), diag_blocks[:, 0], off_blocks[:, 0],
        fluct_state,
    )
    return pl.pallas_call(
        unpack_kernel,
        out_shape=(nodal, nodal, nodal, jax.ShapeDtypeStruct((ELEM, 4 * LEVEL), BF16)),
        in_specs=[VMEM] * 6,
        out_specs=(VMEM, VMEM, VMEM, ANY),
        scratch_shapes=[
            vmem((4, N_DEV, 128), F32),
            vmem((LEVEL, LEVEL), BF16),
            vmem((10, N_DEV, LEVEL), BF16),
            vmem((512, LEVEL), BF16),
            vmem((ELEM, 4 * LEVEL), BF16),
            DMA((4,)),
        ],
        compiler_params=params(None, 60),
        name="unpack",
    )(residual, product, update, tail, body, pmap)


def solution(mesh):
    both = ("sec", "bulk")
    return jax.shard_map(
        on_device,
        mesh=mesh,
        in_specs=(
            P(None, both), P(None, both), P(None, both), P(None, both), P(both), P(both),
            P("bulk", None), P("bulk", None, None), P(None, "bulk", None, None),
            P(None, "bulk", None, None), P(None, "bulk", None), P(None, "bulk", None, None),
            P(None, "bulk"), P(None, "bulk"), P(None, "bulk", None), P("bulk"), P(both, None),
        ),
        out_specs=(P(None, both), P(None, both), P(None, both), P(both, None)),
        check_vma=False,
    )
```

```python
import jax
import jax.numpy as jnp
from jax import lax
from jax.experimental import pallas as pl
from jax.experimental.pallas import tpu as pltpu
from jax.sharding import PartitionSpec as P

F32 = jnp.float32
BF16 = jnp.bfloat16
I32 = jnp.int32
N_DEV = 128
ELEM = 512
NODE = 128
LEVEL = 768
MSG = 64
SWEEPS = 3
ROWS = 20
OFF = 32
MESH = pl.DeviceIdType.MESH
BASE = (0, 6, 18, 36)
SLOT0 = (0, 2, 6, 12)
LEVEL0 = (0, 4, 7, 9)
SKEW_Y = 2
SKEW_Z = 3
EARLY = 14
SPLIT = 8


def dot_nt(a, b):
    return lax.dot_general(a, b, (((1,), (1,)), ((), ())), preferred_element_type=F32)


def dot_nn(a, b):
    return lax.dot_general(a, b, (((1,), (0,)), ((), ())), preferred_element_type=F32)


def iota(shape, dim):
    return lax.broadcasted_iota(I32, shape, dim)


def static_row(c, h, a):
    return SLOT0[c] + h * (c + 1) + a


def my_position():
    sec = lax.axis_index("sec")
    bulk = lax.axis_index("bulk")
    return sec, bulk, sec * 32 + bulk


def wrap(x):
    return x - jnp.where(x >= 4, 4, 0)


def each_peer(sec, bulk, act, core=None, begin=0, end=16):
    bx, bz, bc = bulk // 8, lax.rem(bulk // 2, 4), lax.rem(bulk, 2)
    columns = [wrap(bx + dx) * 8 for dx in range(4)]
    cores = [bc, 1 - bc] if core is None else [core]

    def block(step, first):
        ty0, tz0 = wrap(sec + step // 4), wrap(bz + lax.rem(step, 4))
        for m in range(first, 4 * len(cores)):
            dx = m % 4
            ty = wrap(ty0 + (SKEW_Y * dx) % 4)
            tb = columns[dx] + wrap(tz0 + (SKEW_Z * dx) % 4) * 2 + cores[m // 4]
            act(step, ty, tb, ty * 32 + tb)

    if begin == 0:
        block(jnp.int32(0), 1)

    def body(step, carry):
        block(step, 0)
        return carry

    lax.fori_loop(max(begin, 1), end, body, 0)


def greet_all(barrier, sec, bulk):
    def greet(step, ty, tb, t):
        pl.semaphore_signal(barrier, inc=1, device_id=(ty, tb), device_id_type=MESH)

    each_peer(sec, bulk, greet)


def split3(nodal, scratch):
    high = nodal.astype(BF16).astype(F32)
    rest = nodal - high
    middle = rest.astype(BF16).astype(F32)
    low = rest - middle
    scratch[...] = jnp.zeros_like(scratch)
    rows = nodal.shape[0]
    scratch[0:rows, :] = high
    scratch[8 : 8 + rows, :] = middle
    scratch[16 : 16 + rows, :] = low
    return scratch[...].astype(BF16)


def node_onehot(conn_ref, a):
    ids = conn_ref[a : a + 1, :]
    return jnp.where(iota((NODE, ELEM), 0) == ids, 1.0, 0.0).astype(BF16)


def gather_nodes(nodal, conn_ref, scratch):
    parts = split3(nodal, scratch)
    out = []
    for a in range(4):
        got = dot_nn(parts, node_onehot(conn_ref, a))
        out.append(got[0:8] + got[8:16] + got[16:24])
    return out


def strain_rows(moved, grads_ref):
    g = [[grads_ref[3 * a + k : 3 * a + k + 1, :] for k in range(3)] for a in range(4)]
    u = [[moved[a][k : k + 1, :] for k in range(3)] for a in range(4)]

    def total(terms):
        out = terms[0]
        for t in terms[1:]:
            out = out + t
        return out

    return [
        total([g[a][0] * u[a][0] for a in range(4)]),
        total([g[a][1] * u[a][1] for a in range(4)]),
        total([g[a][2] * u[a][2] for a in range(4)]),
        total([g[a][2] * u[a][1] + g[a][1] * u[a][2] for a in range(4)]),
        total([g[a][2] * u[a][0] + g[a][0] * u[a][2] for a in range(4)]),
        total([g[a][1] * u[a][0] + g[a][0] * u[a][1] for a in range(4)]),
    ]


def make_spread(spread):
    n = iota((1, LEVEL), 1)
    source = lax.rem(n, 128) * 6 + n // 128
    spread[...] = jnp.where(iota((LEVEL, LEVEL), 0) == source, 1.0, 0.0).astype(BF16)


def to_rows(rows):
    n = iota((1, 8 * rows), 1)
    target = lax.rem(n, rows) * 8 + n // rows
    return jnp.where(iota((8 * rows, 8 * rows), 0) == target, 1.0, 0.0).astype(BF16)


def to_slots(rows):
    n = iota((1, 8 * rows), 1)
    target = lax.rem(n, 8) * rows + n // 8
    return jnp.where(iota((8 * rows, 8 * rows), 0) == target, 1.0, 0.0).astype(BF16)


def two_rows(first, second):
    return jnp.concatenate([first, second], axis=0).astype(BF16)


def side_by_side(ref, at, tile):
    parts = [
        ref[pl.ds(at + 8 * i, 8), tile * 16 : tile * 16 + 16, :].reshape(128, 128)
        for i in range(2)
    ]
    return jnp.concatenate(parts, axis=1)


def write_messages(slots, mixed, target, count):
    def lower(g, carry):
        for tile in range(4):
            out = dot_nn(slots, mixed[g, tile * 128 : tile * 128 + 128, :]).astype(BF16)
            for i in range(2):
                target[pl.ds(16 * g + 8 * i, 8), tile * 16 : tile * 16 + 16, :] = out[
                    :, i * 128 : (i + 1) * 128
                ].reshape(8, 16, 128)
        return carry

    lax.fori_loop(0, count, lower, 0, unroll=2)


def prepare_send(strain, pmap, state, ends, mixed, slots, send, spread, flat, srows, load):
    srows[...] = jnp.zeros_like(srows)
    for i in range(6):
        srows[i : i + 1, :] = strain[i]
    where_to = pmap[...]
    owner = where_to // ELEM
    volume = lax.rem(where_to, ELEM) // 64
    srows[8:9, :] = volume.astype(F32)
    strain_low = srows[...].astype(BF16)
    make_spread(spread)
    load.wait()

    ones = jnp.ones((LEVEL, 128), BF16)
    levels = jnp.zeros((ELEM, 128), F32)
    for a in range(4):
        weight = dot_nn(jnp.abs(state[:, a * LEVEL : (a + 1) * LEVEL]), ones)
        levels = jnp.where(weight > 0.0, a + 1.0, levels)
    levels = jnp.transpose(levels)[0:1, :].astype(I32)
    key = (owner * 4096 + levels * 512 + iota((1, ELEM), 1)).astype(F32)
    key_col = jnp.transpose(jnp.broadcast_to(key, (128, ELEM)))
    order = []
    for m in range(4):
        part = key[:, m * 128 : (m + 1) * 128]
        order.append(jnp.sum(jnp.where(key_col < part, 1.0, 0.0), axis=0, keepdims=True))
    order = jnp.concatenate(order, axis=1).astype(I32)

    picks = []
    for k in range(4):
        pick = jnp.where(order == iota((N_DEV, ELEM), 0) * 4 + k, 1.0, 0.0).astype(BF16)
        ends[k] = dot_nt(pick, strain_low)
        picks.append(pick)
    picks = jnp.concatenate(picks, axis=0)
    for a in range(4):
        at, end = LEVEL0[a] * 128, (LEVEL0[a] + 4 - a) * 128
        flat[at:end, :] = dot_nn(
            picks[a * 128 :], state[:, a * LEVEL : (a + 1) * LEVEL]
        ).astype(BF16)
    places = [(k, a) for a in range(4) for k in range(a, 4)]
    for jj in range(3):
        for half in range(2):
            got = dot_nn(
                flat[half * 640 : (half + 1) * 640, :], spread[:, jj * 256 : (jj + 1) * 256]
            )
            for i in range(5):
                k, a = places[half * 5 + i]
                row = BASE[k] + a * 6 + jj * 2
                for ob in range(16):
                    part = got[i * 128 + ob * 8 : i * 128 + ob * 8 + 8]
                    lane = (ob % 2) * 128
                    mixed[ob // 2, row * 8 : row * 8 + 16, lane : lane + 128] = two_rows(
                        part[:, :128], part[:, 128:]
                    )
    for k in (0, 2):
        for ob in range(16):
            lane = (ob % 2) * 128
            at = (60 + k) * 8
            mixed[ob // 2, at : at + 16, lane : lane + 128] = two_rows(
                ends[k, ob * 8 : ob * 8 + 8], ends[k + 1, ob * 8 : ob * 8 + 8]
            )
    slots[...] = to_slots(16)
    write_messages(slots[...], mixed, send, 8)


def make_tables(vols, off_row, off_col, vcls, chrow, ridx, inv, last, prev, crow, ccol, cvol):
    sizes = [vols[0, v] for v in range(8)]
    zero = jnp.int32(0)
    halves, starts, start = [], [], zero
    for v in range(8):
        half = zero
        for w in range(v):
            half = half + jnp.where(sizes[w] == sizes[v], 1, 0)
        halves.append(half)
        starts.append(start)
        start = start + sizes[v]
    for c in range(4):
        for h in range(2):
            vol, first = zero, zero
            for v in range(8):
                hit = (sizes[v] == c + 1) & (halves[v] == h)
                vol = jnp.where(hit, v, vol)
                first = jnp.where(hit, starts[v], first)
            vcls[c * 2 + h] = vol
            for a in range(c + 1):
                ridx[static_row(c, h, a)] = first + a
                chrow[static_row(c, h, a)] = c * 2 + h

    def invert(r, carry):
        found = jnp.int32(0)
        for i in range(ROWS):
            found = jnp.where(ridx[i] == r, i, found)
        inv[r] = found
        return carry

    lax.fori_loop(0, ROWS, invert, 0)

    def ends(c, carry):
        row = inv[off_row[0, c]]
        crow[c] = row
        ccol[c] = inv[off_col[0, c]]
        cvol[c] = chrow[row]
        return carry

    lax.fori_loop(0, OFF, ends, 0)

    def link(c, carry):
        row = crow[c]
        before = jnp.int32(0)
        for k in range(OFF):
            before = jnp.where((crow[k] == row) & (k < c), k + 1, before)
        prev[c] = before
        return carry

    lax.fori_loop(0, OFF, link, 0)

    def finish(i, carry):
        end = jnp.int32(0)
        for k in range(OFF):
            end = jnp.where(crow[k] == i, k + 1, end)
        last[i] = end
        return carry

    lax.fori_loop(0, ROWS, finish, 0)


def step_kernel(
    disp, load_ref, conn, grads, volume_ref, pmap, vols, affine, diag_n, off_n, off_row,
    off_col, off_count, coupling_hbm, diag_hbm, off_hbm, state_hbm,
    tail, body, residual_ref, product_ref, update_ref,
    fluct, ends, mixed, slots, rows_of, turned, send, spread, flat, srows, small, small_e,
    got, back, coupling, diag, off,
    state, low, chain, mask, strain, rdiag, cscale, dinv, weights, aff,
    tails, parts, mine, norms,
    vcls, chrow, ridx, inv, last, prev, crow, ccol, cvol,
    load_sems, own_sems, go_send, go_recv, tail_send, tail_recv, body_send, body_recv,
    norm_send, norm_recv,
):
    sec, bulk, me = my_position()
    core = lax.rem(bulk, 2)
    barrier = pltpu.get_barrier_semaphore()
    loads = []
    for i, (source, target) in enumerate(
        [(state_hbm, fluct), (off_hbm, off), (diag_hbm, diag), (coupling_hbm, coupling)]
    ):
        loads.append(pltpu.make_async_copy(source, target, load_sems.at[i]))
        loads[-1].start()
    greet_all(barrier, sec, bulk)
    macro = strain_rows(gather_nodes(disp[...], conn, small), grads)
    prepare_send(macro, pmap, fluct, ends, mixed, slots, send, spread, flat, srows, loads[0])
    own = pltpu.make_async_copy(send.at[me], got.at[core, me // 2], own_sems.at[0])
    own.start()
    pl.semaphore_wait(barrier, N_DEV - 1)

    def push(step, ty, tb, t):
        late = jnp.where(step >= EARLY, 1, 0)
        pltpu.make_async_remote_copy(
            src_ref=send.at[t],
            dst_ref=got.at[core, me // 2],
            send_sem=go_send,
            recv_sem=go_recv.at[core, late],
            device_id=(ty, tb),
            device_id_type=MESH,
        ).start()

    @pl.when(core == 0)
    def _():
        each_peer(sec, bulk, push)

    make_tables(vols, off_row, off_col, vcls, chrow, ridx, inv, last, prev, crow, ccol, cvol)
    lanes6 = iota((36, 128), 1)
    rows6 = iota((36, 128), 0)
    place = jnp.where(lanes6 == lax.rem(rows6, 6) * 8 + rows6 // 6, 1.0, 0.0).astype(F32)
    spread_affine = lax.dot_general(
        affine[0], place, (((1,), (0,)), ((), ())),
        preferred_element_type=F32, precision=lax.Precision.HIGHEST,
    )
    for v in range(8):
        aff[v] = spread_affine[v : v + 1, :]
    eye = iota((128, 128), 0) == iota((128, 128), 1)
    for load in loads[1:]:
        load.wait()

    def prepare(i, carry):
        r = ridx[i]
        values = jnp.where(eye, diag[r].astype(F32), 0.0)
        dinv[i] = 1.0 / jnp.sum(values, axis=0, keepdims=True)
        load = coupling[r].reshape(6, 128)
        high = load.astype(BF16).astype(F32)
        block = jnp.zeros((58, 128), F32)
        weights[i] = jnp.concatenate([high, block, load - high, block], axis=0).astype(BF16)
        return carry

    lax.fori_loop(0, ROWS, prepare, 0, unroll=2)
    rows_of[...] = to_rows(16)
    chain[0] = jnp.zeros((192, 128), F32)
    live = off_count[0]
    own.wait()

    partner = bulk + 1 - 2 * core

    def send_back(p, first, rows, target, send_sem, recv_sem, begin=0, end=16):
        def push_back(step, ty, tb, t):
            pltpu.make_async_remote_copy(
                src_ref=back.at[p, t // 2, pl.ds(first, rows)],
                dst_ref=target.at[me],
                send_sem=send_sem,
                recv_sem=recv_sem,
                device_id=(ty, tb),
                device_id_type=MESH,
            ).start()

        each_peer(sec, bulk, push_back, p, begin, end)
        if begin == 0:

            @pl.when(core != p)
            def _():
                push_back(0, sec, partner, sec * 32 + partner)

    def phase(p, carry):
        early = 4 * EARLY

        @pl.when(core == p)
        def _():
            part = got.at[p, pl.ds(0, early - 1)]
            pltpu.make_async_copy(part, part, go_recv.at[p, 0]).wait()

        @pl.when(core != p)
        def _():
            part = got.at[p, pl.ds(0, early)]
            pltpu.make_async_copy(part, part, go_recv.at[p, 0]).wait()

        @pl.when((p == 0) & (core == 1))
        def _():
            each_peer(sec, bulk, push)

        part = got.at[p, pl.ds(0, 64 - early)]
        pltpu.make_async_copy(part, part, go_recv.at[p, 1]).wait()

        def take(g, c2):
            h = g // 2
            q0 = pl.multiple_of(lax.rem(g, 2) * 16, 16)
            for tile in range(4):
                turned[tile * 128 : tile * 128 + 128, :] = dot_nn(
                    rows_of[...], side_by_side(got.at[p], 16 * g, tile)
                )

            def message_row(r):
                part = turned[r * 8 : r * 8 + 8, :]
                return jnp.concatenate([part[:, :128], part[:, 128:]], axis=0)

            rest = [message_row(60 + k) for k in range(4)]
            for c in range(4):
                v = vcls[c * 2 + h].astype(F32)
                picked = jnp.zeros((16, 128), F32)
                for k in range(4):
                    code = jnp.broadcast_to(rest[k][:, 8:9], (16, 128))
                    m = jnp.where(code == v, 1.0, 0.0)
                    mask[c * 4 + k] = m
                    picked = picked + m * rest[k]
                for i in range(6):
                    strain[(c * 2 + h) * 6 + i, pl.ds(q0, 16), :] = jnp.broadcast_to(
                        picked[:, i : i + 1], (16, 128)
                    )
            for a in range(4):
                for j in range(6):
                    sums = {}
                    for k in range(a, 4):
                        part = message_row(BASE[k] + a * 6 + j)
                        for c in range(a, 4):
                            term = mask[c * 4 + k] * part
                            sums[c] = sums[c] + term if c in sums else term
                    for c in range(a, 4):
                        i = static_row(c, h, a)
                        at = pl.multiple_of(j * 32 + q0, 16)
                        state[i, pl.ds(at, 16), :] = sums[c]
                        low[i, pl.ds(at, 16), :] = sums[c].astype(BF16)
            return c2

        lax.fori_loop(0, 4, take, 0)

        def row_scale(i, c2):
            r = ridx[i]
            ch = chrow[i] * 6
            z = diag_n[0, 0, r] * strain[ch]
            for k in range(1, 6):
                z = z + diag_n[k, 0, r] * strain[ch + k]
            rdiag[i] = 1.0 / (1.0 + 0.4 * jnp.tanh(z))
            return c2

        lax.fori_loop(0, ROWS, row_scale, 0, unroll=5)

        def contact_scale(c, c2):
            ch = cvol[c] * 6
            z = off_n[0, 0, c] * strain[ch]
            for k in range(1, 6):
                z = z + off_n[k, 0, c] * strain[ch + k]
            on = jnp.where(c < live, 1.0, 0.0).astype(F32)
            cscale[c] = (1.0 + 0.4 * jnp.tanh(z)) * on
            return c2

        lax.fori_loop(0, OFF, contact_scale, 0, unroll=8)

        def sweep(n, c2):
            def contact(c, c3):
                value = dot_nt(low[ccol[c]], off[c]).reshape(6, 32, 128)
                scaled = (value * cscale[c][None]).reshape(192, 128)
                chain[c + 1] = chain[prev[c]] + scaled
                return c3

            lax.fori_loop(0, OFF, contact, 0, unroll=16)

            def update(i, c3):
                r = ridx[i]
                own_part = dot_nt(low[i], diag[r]).reshape(6, 32, 128)
                extra = chain[last[i]].reshape(6, 32, 128)
                step = ((coupling[r] - extra) * rdiag[i][None] - own_part) * dinv[i][None]
                new = state[i] + step.reshape(192, 128)
                state[i] = new
                low[i] = new.astype(BF16)
                return c3

            lax.fori_loop(0, ROWS, update, 0, unroll=10)
            return c2

        lax.fori_loop(0, SWEEPS, sweep, 0)

        lane = iota((32, 128), 1)
        for h in range(2):
            last_rows = []
            for c in range(4):
                acc = jnp.zeros((192, 128), F32)
                for a in range(c + 1):
                    i = static_row(c, h, a)
                    x = state[i]
                    high = low[i]
                    acc = acc + dot_nt(high, weights[i])
                    acc = acc + dot_nt((x - high.astype(F32)).astype(BF16), weights[i])
                    for j in range(0, 6, 2):
                        at = (BASE[c] + a * 6 + j) * 8
                        for q in range(4):
                            cols = (q % 2) * 128
                            mixed[h * 2 + q // 2, at : at + 16, cols : cols + 128] = two_rows(
                                x[j * 32 + q * 8 : j * 32 + q * 8 + 8],
                                x[j * 32 + 32 + q * 8 : j * 32 + 40 + q * 8],
                            )
                t = acc[0:32]
                for j in range(1, 6):
                    t = t + pltpu.roll(acc[j * 32 : (j + 1) * 32], 8 * j, axis=1)
                t = t + pltpu.roll(t, 64, axis=1)
                v = vcls[c * 2 + h]
                tangent = aff[v] - t / (128.0 * (c + 1))
                last_rows.append(
                    jnp.where(lane < 48, tangent, jnp.where(lane == 64, v.astype(F32), 0.0))
                )
            for k in (0, 2):
                at = (60 + k) * 8
                for q in range(4):
                    cols = (q % 2) * 128
                    mixed[h * 2 + q // 2, at : at + 16, cols : cols + 128] = two_rows(
                        last_rows[k][q * 8 : q * 8 + 8], last_rows[k + 1][q * 8 : q * 8 + 8]
                    )

        write_messages(slots[...], mixed, back.at[p], 4)

        send_back(p, 48, 16, tails, tail_send, tail_recv)

        @pl.when(p == 0)
        def _():
            send_back(0, 0, 48, body, body_send, body_recv, 0, SPLIT)

        return carry

    lax.fori_loop(0, 2, phase, 0)
    send_back(0, 0, 48, body, body_send, body_recv, SPLIT, 16)
    mine_back = back.at[core, me // 2]
    own_tail = pltpu.make_async_copy(mine_back.at[pl.ds(48, 16)], tails.at[me], own_sems.at[0])
    own_body = pltpu.make_async_copy(mine_back.at[pl.ds(0, 48)], body.at[me], own_sems.at[1])
    own_tail.start()
    own_body.start()

    where_to = pmap[...]
    owner = where_to // ELEM
    volume = (lax.rem(where_to, ELEM) // 64).astype(F32)
    same_owner = iota((N_DEV, ELEM), 0) == owner
    own_tail.wait()
    landed = tails.at[pl.ds(0, N_DEV - 1)]
    pltpu.make_async_copy(landed, landed, tail_recv).wait()
    keep = pltpu.make_async_copy(tails, tail, own_sems.at[2])
    keep.start()
    turn = to_rows(16)[96:128]
    for g in range(8):
        out = dot_nn(turn, side_by_side(tails, 16 * g, 0))
        for c in range(4):
            for i in range(2):
                parts[c, 16 * g + 8 * i : 16 * g + 8 * i + 8, :] = out[
                    c * 8 : c * 8 + 8, i * 128 : (i + 1) * 128
                ]
    tangent = jnp.zeros((128, ELEM), F32)
    for c in range(4):
        part = parts[c]
        code = jnp.broadcast_to(part[:, 64:65], (N_DEV, ELEM))
        pick = jnp.where(same_owner & (code == volume), 1.0, 0.0).astype(BF16)
        tangent = tangent + dot_nn(jnp.transpose(part).astype(BF16), pick)
    weight = volume_ref[...]
    macro_rows = [srows[i : i + 1, :] for i in range(6)]
    residual = (
        assemble(grads, conn, apply_tangent(tangent, macro_rows, weight), small_e) - load_ref[...]
    )
    residual_ref[...] = residual
    mine[...] = jnp.broadcast_to(
        jnp.sum(jnp.sum(residual * residual, axis=1, keepdims=True), axis=0, keepdims=True),
        (1, 128),
    )
    norms[me] = mine[...]

    def push_norm(step, ty, tb, t):
        pltpu.make_async_remote_copy(
            src_ref=mine,
            dst_ref=norms.at[me],
            send_sem=norm_send,
            recv_sem=norm_recv,
            device_id=(ty, tb),
            device_id_type=MESH,
        ).start()

    each_peer(sec, bulk, push_norm)
    send_back(1, 0, 48, body, body_send, body_recv)
    trial = strain_rows(gather_nodes(residual, conn, small), grads)
    product_ref[...] = assemble(grads, conn, apply_tangent(tangent, trial, weight), small_e)
    arrived = norms.at[pl.ds(0, N_DEV - 1)]
    pltpu.make_async_copy(arrived, arrived, norm_recv).wait()
    total = jnp.sum(norms[...], axis=0)
    root = jnp.sqrt(total / (3.0 * 16384) + 1e-06)
    update_ref[...] = -jnp.minimum(1.0, 1.0 / root) * residual

    sent = send.at[pl.ds(0, N_DEV - 1)]
    pltpu.make_async_copy(sent, sent, go_send).wait()
    pltpu.make_async_copy(arrived, arrived, norm_send).wait()
    keep.wait()
    own_body.wait()
    pltpu.make_async_copy(landed, landed, tail_send).wait()
    rest = body.at[pl.ds(0, N_DEV - 1)]
    pltpu.make_async_copy(rest, rest, body_send).wait()
    pltpu.make_async_copy(rest, rest, body_recv).wait()


def unpack_kernel(
    residual, product, update, tail_hbm, body_hbm, pmap,
    out_residual, out_product, out_update, out_hbm,
    tail, body, parts, spread, rows, flat, result, load_sems, sems,
):
    loads = [
        pltpu.make_async_copy(tail_hbm, tail, load_sems.at[0]),
        pltpu.make_async_copy(body_hbm, body, load_sems.at[1]),
    ]
    for load in loads:
        load.start()
    out_residual[...] = residual[...]
    out_product[...] = product[...]
    out_update[...] = update[...]
    n = iota((1, LEVEL), 1)
    source = lax.rem(n, 6) * 128 + n // 6
    spread[...] = jnp.where(iota((LEVEL, LEVEL), 0) == source, 1.0, 0.0).astype(BF16)
    turn = to_rows(16)
    where_to = pmap[...].astype(F32)
    column = jnp.transpose(jnp.broadcast_to(where_to, (128, ELEM))).astype(I32)
    owner = column // ELEM
    volume = lax.rem(column, ELEM) // 64
    same_owner = iota((ELEM, N_DEV), 1) == owner
    for load in loads:
        load.wait()
    for tile in range(4):
        for g in range(8):
            source_ref, at = (body, tile) if tile < 3 else (tail, 0)
            got = dot_nn(turn, side_by_side(source_ref, 16 * g, at))
            for i in range(16):
                r = tile * 16 + i
                part = got[i * 8 : i * 8 + 8]
                if r < 60:
                    c = 0 if r < 6 else 1 if r < 18 else 2 if r < 36 else 3
                    a, j = (r - BASE[c]) // 6, r % 6
                    block = LEVEL0[a] + c - a
                    rows[
                        block * 128 + 16 * g : block * 128 + 16 * g + 16, j * 128 : (j + 1) * 128
                    ] = two_rows(part[:, :128], part[:, 128:])
                else:
                    for side in range(2):
                        parts[r - 60, 16 * g + 8 * side : 16 * g + 8 * side + 8, :] = part[
                            :, side * 128 : (side + 1) * 128
                        ]
    picks = []
    for c in range(4):
        code = jnp.transpose(parts[c])[64:65, :].astype(I32)
        picks.append(jnp.where(same_owner & (code == volume), 1.0, 0.0).astype(BF16))
    pick = jnp.concatenate(picks, axis=1)
    copies = []
    for a in range(4):
        at, end = LEVEL0[a] * 128, (LEVEL0[a] + 4 - a) * 128
        flat[at:end, :] = dot_nn(rows[at:end, :], spread[...]).astype(BF16)
        result[:, a * LEVEL : (a + 1) * LEVEL] = dot_nn(
            pick[:, a * 128 :], flat[at:end, :]
        ).astype(BF16)
        part = pl.ds(a * LEVEL, LEVEL)
        copy = pltpu.make_async_copy(result.at[:, part], out_hbm.at[:, part], sems.at[a])
        copy.start()
        copies.append(copy)
    for copy in copies:
        copy.wait()


def forces_of(grads_ref, s):
    g = [[grads_ref[3 * a + k : 3 * a + k + 1, :] for k in range(3)] for a in range(4)]
    out = []
    for a in range(4):
        gx, gy, gz = g[a]
        out.append(
            (
                gx * s[0] + gz * s[4] + gy * s[5],
                gy * s[1] + gz * s[3] + gx * s[5],
                gz * s[2] + gy * s[3] + gx * s[4],
            )
        )
    return out


def assemble(grads_ref, conn_ref, stress, scratch):
    forces = forces_of(grads_ref, stress)
    total = jnp.zeros((8, NODE), F32)
    for a in range(4):
        scratch[...] = jnp.zeros_like(scratch)
        for k in range(3):
            f = forces[a][k]
            high = f.astype(BF16).astype(F32)
            rest = f - high
            middle = rest.astype(BF16).astype(F32)
            scratch[k : k + 1, :] = high
            scratch[8 + k : 9 + k, :] = middle
            scratch[16 + k : 17 + k, :] = rest - middle
        part = dot_nt(scratch[...].astype(BF16), node_onehot(conn_ref, a))
        total = total + (part[0:8] + part[8:16] + part[16:24])
    return total[0:3]


def apply_tangent(tangent, strain, weight):
    acc = tangent[0:8] * strain[0]
    for j in range(1, 6):
        acc = acc + tangent[8 * j : 8 * j + 8] * strain[j]
    acc = acc * weight
    return [acc[i : i + 1, :] for i in range(6)]


VMEM = pl.BlockSpec(memory_space=pltpu.VMEM)
SMEM = pl.BlockSpec(memory_space=pltpu.SMEM)
ANY = pl.BlockSpec(memory_space=pl.ANY)
DMA = pltpu.SemaphoreType.DMA


def params(collective_id=None, limit=48):
    return pltpu.CompilerParams(
        collective_id=collective_id,
        has_side_effects=collective_id is not None,
        vmem_limit_bytes=limit * 2**20,
    )


def on_device(
    displacement, nodal_load, connectivity, shape_grads, elem_volume, point_map, vol_blocks,
    c_affine, coupling, diag_blocks, diag_normal, off_blocks, off_row, off_col, off_normal,
    off_count, fluct_state,
):
    pmap = point_map.reshape(1, ELEM)
    volume = elem_volume.reshape(1, ELEM)
    smem = lambda n: pltpu.SMEM((n,), I32)
    vmem = pltpu.VMEM
    nodal = jax.ShapeDtypeStruct((3, NODE), F32)
    tail, body, residual, product, update = pl.pallas_call(
        step_kernel,
        out_shape=(
            jax.ShapeDtypeStruct((N_DEV, 16, 128), BF16),
            jax.ShapeDtypeStruct((N_DEV, 48, 128), BF16),
            nodal, nodal, nodal,
        ),
        in_specs=[VMEM] * 6 + [SMEM, VMEM] + [SMEM] * 5 + [ANY] * 4,
        out_specs=(ANY, ANY, VMEM, VMEM, VMEM),
        scratch_shapes=[
            vmem((ELEM, 4 * LEVEL), BF16),
            vmem((4, N_DEV, 128), F32),
            vmem((8, 512, 256), BF16),
            vmem((128, 128), BF16),
            vmem((128, 128), BF16),
            vmem((512, 256), F32),
            vmem((N_DEV, MSG, 128), BF16),
            vmem((LEVEL, LEVEL), BF16),
            vmem((1280, LEVEL), BF16),
            vmem((128, ELEM), F32),
            vmem((32, 128), F32),
            vmem((32, ELEM), F32),
            vmem((2, 64, MSG, 128), BF16),
            vmem((2, 64, MSG, 128), BF16),
            vmem((ROWS, 6, 1, 128), F32),
            vmem((ROWS, 128, 128), BF16),
            vmem((OFF, 128, 128), BF16),
            vmem((ROWS, 192, 128), F32),
            vmem((ROWS, 192, 128), BF16),
            vmem((OFF + 1, 192, 128), F32),
            vmem((16, 16, 128), F32),
            vmem((48, 32, 128), F32),
            vmem((ROWS, 32, 128), F32),
            vmem((OFF, 32, 128), F32),
            vmem((ROWS, 1, 128), F32),
            vmem((ROWS, 128, 128), BF16),
            vmem((8, 1, 128), F32),
            vmem((N_DEV, 16, 128), BF16),
            vmem((4, N_DEV, 128), F32),
            vmem((1, 128), F32),
            vmem((N_DEV, 1, 128), F32),
            smem(8), smem(ROWS), smem(ROWS), smem(ROWS), smem(ROWS),
            smem(OFF), smem(OFF), smem(OFF), smem(OFF),
            DMA((4,)), DMA((3,)), DMA, DMA((2, 2)), DMA, DMA, DMA, DMA, DMA, DMA,
        ],
        compiler_params=params(1, 60),
        name="step",
    )(
        displacement, nodal_load, connectivity, shape_grads, volume, pmap, vol_blocks, c_affine,
        diag_normal.transpose(2, 1, 0), off_normal.transpose(2, 1, 0), off_row.T, off_col.T,
        off_count, coupling.transpose(0, 2, 1, 3), diag_blocks[:, 0], off_blocks[:, 0],
        fluct_state,
    )
    return pl.pallas_call(
        unpack_kernel,
        out_shape=(nodal, nodal, nodal, jax.ShapeDtypeStruct((ELEM, 4 * LEVEL), BF16)),
        in_specs=[VMEM, VMEM, VMEM, ANY, ANY, VMEM],
        out_specs=(VMEM, VMEM, VMEM, ANY),
        scratch_shapes=[
            vmem((N_DEV, 16, 128), BF16),
            vmem((N_DEV, 48, 128), BF16),
            vmem((4, N_DEV, 128), F32),
            vmem((LEVEL, LEVEL), BF16),
            vmem((1280, LEVEL), BF16),
            vmem((1280, LEVEL), BF16),
            vmem((ELEM, 4 * LEVEL), BF16),
            DMA((2,)),
            DMA((4,)),
        ],
        compiler_params=params(None, 60),
        name="unpack",
    )(residual, product, update, tail, body, pmap)


def solution(mesh):
    both = ("sec", "bulk")
    return jax.shard_map(
        on_device,
        mesh=mesh,
        in_specs=(
            P(None, both), P(None, both), P(None, both), P(None, both), P(both), P(both),
            P("bulk", None), P("bulk", None, None), P(None, "bulk", None, None),
            P(None, "bulk", None, None), P(None, "bulk", None), P(None, "bulk", None, None),
            P(None, "bulk"), P(None, "bulk"), P(None, "bulk", None), P("bulk"), P(both, None),
        ),
        out_specs=(P(None, both), P(None, both), P(None, both), P(both, None)),
        check_vma=False,
    )
```

```python
import jax
import jax.numpy as jnp
from jax import lax
from jax.experimental import pallas as pl
from jax.experimental.pallas import tpu as pltpu
from jax.sharding import PartitionSpec as P

F32 = jnp.float32
BF16 = jnp.bfloat16
I32 = jnp.int32
N_DEV = 128
ELEM = 512
NODE = 128
LEVEL = 768
MSG = 64
SWEEPS = 3
ROWS = 20
OFF = 32
MESH = pl.DeviceIdType.MESH
BASE = (0, 6, 18, 36)
SLOT0 = (0, 2, 6, 12)
LEVEL0 = (0, 4, 7, 9)
SKEW_Y = 2
SKEW_Z = 3
EARLY = 14
SPLIT = 8


def dot_nt(a, b):
    return lax.dot_general(a, b, (((1,), (1,)), ((), ())), preferred_element_type=F32)


def dot_nn(a, b):
    return lax.dot_general(a, b, (((1,), (0,)), ((), ())), preferred_element_type=F32)


def iota(shape, dim):
    return lax.broadcasted_iota(I32, shape, dim)


def static_row(c, h, a):
    return SLOT0[c] + h * (c + 1) + a


def my_position():
    sec = lax.axis_index("sec")
    bulk = lax.axis_index("bulk")
    return sec, bulk, sec * 32 + bulk


def wrap(x):
    return x - jnp.where(x >= 4, 4, 0)


def each_peer(sec, bulk, act, core=None, begin=0, end=16):
    bx, bz, bc = bulk // 8, lax.rem(bulk // 2, 4), lax.rem(bulk, 2)
    columns = [wrap(bx + dx) * 8 for dx in range(4)]
    cores = [bc, 1 - bc] if core is None else [core]

    def block(step, first):
        ty0, tz0 = wrap(sec + step // 4), wrap(bz + lax.rem(step, 4))
        for m in range(first, 4 * len(cores)):
            dx = m % 4
            ty = wrap(ty0 + (SKEW_Y * dx) % 4)
            tb = columns[dx] + wrap(tz0 + (SKEW_Z * dx) % 4) * 2 + cores[m // 4]
            act(step, ty, tb, ty * 32 + tb)

    if begin == 0:
        block(jnp.int32(0), 1)

    def body(step, carry):
        block(step, 0)
        return carry

    lax.fori_loop(max(begin, 1), end, body, 0)


def greet_all(barrier, sec, bulk):
    def greet(step, ty, tb, t):
        pl.semaphore_signal(barrier, inc=1, device_id=(ty, tb), device_id_type=MESH)

    each_peer(sec, bulk, greet)


def split3(nodal, scratch):
    high = nodal.astype(BF16).astype(F32)
    rest = nodal - high
    middle = rest.astype(BF16).astype(F32)
    low = rest - middle
    scratch[...] = jnp.zeros_like(scratch)
    rows = nodal.shape[0]
    scratch[0:rows, :] = high
    scratch[8 : 8 + rows, :] = middle
    scratch[16 : 16 + rows, :] = low
    return scratch[...].astype(BF16)


def node_onehot(conn_ref, a):
    ids = conn_ref[a : a + 1, :]
    return jnp.where(iota((NODE, ELEM), 0) == ids, 1.0, 0.0).astype(BF16)


def gather_nodes(nodal, conn_ref, scratch):
    parts = split3(nodal, scratch)
    out = []
    for a in range(4):
        got = dot_nn(parts, node_onehot(conn_ref, a))
        out.append(got[0:8] + got[8:16] + got[16:24])
    return out


def strain_rows(moved, grads_ref):
    g = [[grads_ref[3 * a + k : 3 * a + k + 1, :] for k in range(3)] for a in range(4)]
    u = [[moved[a][k : k + 1, :] for k in range(3)] for a in range(4)]

    def total(terms):
        out = terms[0]
        for t in terms[1:]:
            out = out + t
        return out

    return [
        total([g[a][0] * u[a][0] for a in range(4)]),
        total([g[a][1] * u[a][1] for a in range(4)]),
        total([g[a][2] * u[a][2] for a in range(4)]),
        total([g[a][2] * u[a][1] + g[a][1] * u[a][2] for a in range(4)]),
        total([g[a][2] * u[a][0] + g[a][0] * u[a][2] for a in range(4)]),
        total([g[a][1] * u[a][0] + g[a][0] * u[a][1] for a in range(4)]),
    ]


def make_spread(spread):
    n = iota((1, LEVEL), 1)
    source = lax.rem(n, 128) * 6 + n // 128
    spread[...] = jnp.where(iota((LEVEL, LEVEL), 0) == source, 1.0, 0.0).astype(BF16)


def to_rows(rows):
    n = iota((1, 8 * rows), 1)
    target = lax.rem(n, rows) * 8 + n // rows
    return jnp.where(iota((8 * rows, 8 * rows), 0) == target, 1.0, 0.0).astype(BF16)


def to_slots(rows):
    n = iota((1, 8 * rows), 1)
    target = lax.rem(n, 8) * rows + n // 8
    return jnp.where(iota((8 * rows, 8 * rows), 0) == target, 1.0, 0.0).astype(BF16)


def two_rows(first, second):
    return jnp.concatenate([first, second], axis=0).astype(BF16)


def side_by_side(ref, at, tile):
    parts = [
        ref[pl.ds(at + 8 * i, 8), tile * 16 : tile * 16 + 16, :].reshape(128, 128)
        for i in range(2)
    ]
    return jnp.concatenate(parts, axis=1)


def write_messages(slots, mixed, target, count):
    def lower(g, carry):
        for tile in range(4):
            out = dot_nn(slots, mixed[g, tile * 128 : tile * 128 + 128, :]).astype(BF16)
            for i in range(2):
                target[pl.ds(16 * g + 8 * i, 8), tile * 16 : tile * 16 + 16, :] = out[
                    :, i * 128 : (i + 1) * 128
                ].reshape(8, 16, 128)
        return carry

    lax.fori_loop(0, count, lower, 0, unroll=4)


def prepare_send(strain, pmap, state, ends, mixed, slots, send, spread, flat, srows, load):
    srows[...] = jnp.zeros_like(srows)
    for i in range(6):
        srows[i : i + 1, :] = strain[i]
    where_to = pmap[...]
    owner = where_to // ELEM
    volume = lax.rem(where_to, ELEM) // 64
    srows[8:9, :] = volume.astype(F32)
    strain_low = srows[...].astype(BF16)
    make_spread(spread)
    load.wait()

    ones = jnp.ones((LEVEL, 128), BF16)
    levels = jnp.zeros((ELEM, 128), F32)
    for a in range(4):
        weight = dot_nn(jnp.abs(state[:, a * LEVEL : (a + 1) * LEVEL]), ones)
        levels = jnp.where(weight > 0.0, a + 1.0, levels)
    levels = jnp.transpose(levels)[0:1, :].astype(I32)
    key = (owner * 4096 + levels * 512 + iota((1, ELEM), 1)).astype(F32)
    key_col = jnp.transpose(jnp.broadcast_to(key, (128, ELEM)))
    order = []
    for m in range(4):
        part = key[:, m * 128 : (m + 1) * 128]
        order.append(jnp.sum(jnp.where(key_col < part, 1.0, 0.0), axis=0, keepdims=True))
    order = jnp.concatenate(order, axis=1).astype(I32)

    picks = []
    for k in range(4):
        pick = jnp.where(order == iota((N_DEV, ELEM), 0) * 4 + k, 1.0, 0.0).astype(BF16)
        ends[k] = dot_nt(pick, strain_low)
        picks.append(pick)
    picks = jnp.concatenate(picks, axis=0)
    for a in range(4):
        at, end = LEVEL0[a] * 128, (LEVEL0[a] + 4 - a) * 128
        flat[at:end, :] = dot_nn(
            picks[a * 128 :], state[:, a * LEVEL : (a + 1) * LEVEL]
        ).astype(BF16)
    places = [(k, a) for a in range(4) for k in range(a, 4)]
    for jj in range(3):
        for half in range(2):
            got = dot_nn(
                flat[half * 640 : (half + 1) * 640, :], spread[:, jj * 256 : (jj + 1) * 256]
            )
            for i in range(5):
                k, a = places[half * 5 + i]
                row = BASE[k] + a * 6 + jj * 2
                for ob in range(16):
                    part = got[i * 128 + ob * 8 : i * 128 + ob * 8 + 8]
                    lane = (ob % 2) * 128
                    mixed[ob // 2, row * 8 : row * 8 + 16, lane : lane + 128] = two_rows(
                        part[:, :128], part[:, 128:]
                    )
    for k in (0, 2):
        for ob in range(16):
            lane = (ob % 2) * 128
            at = (60 + k) * 8
            mixed[ob // 2, at : at + 16, lane : lane + 128] = two_rows(
                ends[k, ob * 8 : ob * 8 + 8], ends[k + 1, ob * 8 : ob * 8 + 8]
            )
    slots[...] = to_slots(16)
    write_messages(slots[...], mixed, send, 8)


def make_tables(vols, off_row, off_col, vcls, chrow, ridx, inv, last, prev, crow, ccol, cvol):
    sizes = [vols[0, v] for v in range(8)]
    zero = jnp.int32(0)
    halves, starts, start = [], [], zero
    for v in range(8):
        half = zero
        for w in range(v):
            half = half + jnp.where(sizes[w] == sizes[v], 1, 0)
        halves.append(half)
        starts.append(start)
        start = start + sizes[v]
    for c in range(4):
        for h in range(2):
            vol, first = zero, zero
            for v in range(8):
                hit = (sizes[v] == c + 1) & (halves[v] == h)
                vol = jnp.where(hit, v, vol)
                first = jnp.where(hit, starts[v], first)
            vcls[c * 2 + h] = vol
            for a in range(c + 1):
                ridx[static_row(c, h, a)] = first + a
                chrow[static_row(c, h, a)] = c * 2 + h

    def invert(r, carry):
        found = jnp.int32(0)
        for i in range(ROWS):
            found = jnp.where(ridx[i] == r, i, found)
        inv[r] = found
        return carry

    lax.fori_loop(0, ROWS, invert, 0)

    def ends(c, carry):
        row = inv[off_row[0, c]]
        crow[c] = row
        ccol[c] = inv[off_col[0, c]]
        cvol[c] = chrow[row]
        return carry

    lax.fori_loop(0, OFF, ends, 0)

    def link(c, carry):
        row = crow[c]
        before = jnp.int32(0)
        for k in range(OFF):
            before = jnp.where((crow[k] == row) & (k < c), k + 1, before)
        prev[c] = before
        return carry

    lax.fori_loop(0, OFF, link, 0)

    def finish(i, carry):
        end = jnp.int32(0)
        for k in range(OFF):
            end = jnp.where(crow[k] == i, k + 1, end)
        last[i] = end
        return carry

    lax.fori_loop(0, ROWS, finish, 0)


def step_kernel(
    disp, load_ref, conn, grads, volume_ref, pmap, vols, affine, diag_n, off_n, off_row,
    off_col, off_count, coupling_hbm, diag_hbm, off_hbm, state_hbm,
    tail, body, residual_ref, product_ref, update_ref,
    fluct, ends, mixed, slots, rows_of, turned, send, spread, flat, srows, small, small_e,
    got, back, coupling, diag, off,
    state, low, chain, mask, strain, rdiag, cscale, dinv, weights, aff,
    tails, parts, mine, norms,
    vcls, chrow, ridx, inv, last, prev, crow, ccol, cvol,
    load_sems, own_sems, go_send, go_recv, tail_send, tail_recv, body_send, body_recv,
    norm_send, norm_recv,
):
    sec, bulk, me = my_position()
    core = lax.rem(bulk, 2)
    barrier = pltpu.get_barrier_semaphore()
    loads = []
    for i, (source, target) in enumerate(
        [(state_hbm, fluct), (off_hbm, off), (diag_hbm, diag), (coupling_hbm, coupling)]
    ):
        loads.append(pltpu.make_async_copy(source, target, load_sems.at[i]))
        loads[-1].start()
    greet_all(barrier, sec, bulk)
    macro = strain_rows(gather_nodes(disp[...], conn, small), grads)
    prepare_send(macro, pmap, fluct, ends, mixed, slots, send, spread, flat, srows, loads[0])
    own = pltpu.make_async_copy(send.at[me], got.at[core, me // 2], own_sems.at[0])
    own.start()
    pl.semaphore_wait(barrier, N_DEV - 1)

    def push(step, ty, tb, t):
        late = jnp.where(step >= EARLY, 1, 0)
        pltpu.make_async_remote_copy(
            src_ref=send.at[t],
            dst_ref=got.at[core, me // 2],
            send_sem=go_send,
            recv_sem=go_recv.at[core, late],
            device_id=(ty, tb),
            device_id_type=MESH,
        ).start()

    @pl.when(core == 0)
    def _():
        each_peer(sec, bulk, push)

    make_tables(vols, off_row, off_col, vcls, chrow, ridx, inv, last, prev, crow, ccol, cvol)
    lanes6 = iota((36, 128), 1)
    rows6 = iota((36, 128), 0)
    place = jnp.where(lanes6 == lax.rem(rows6, 6) * 8 + rows6 // 6, 1.0, 0.0).astype(F32)
    spread_affine = lax.dot_general(
        affine[0], place, (((1,), (0,)), ((), ())),
        preferred_element_type=F32, precision=lax.Precision.HIGHEST,
    )
    for v in range(8):
        aff[v] = spread_affine[v : v + 1, :]
    eye = iota((128, 128), 0) == iota((128, 128), 1)
    for load in loads[1:]:
        load.wait()

    def prepare(i, carry):
        r = ridx[i]
        values = jnp.where(eye, diag[r].astype(F32), 0.0)
        dinv[i] = 1.0 / jnp.sum(values, axis=0, keepdims=True)
        load = coupling[r].reshape(6, 128)
        high = load.astype(BF16).astype(F32)
        block = jnp.zeros((58, 128), F32)
        weights[i] = jnp.concatenate([high, block, load - high, block], axis=0).astype(BF16)
        return carry

    lax.fori_loop(0, ROWS, prepare, 0, unroll=2)
    rows_of[...] = to_rows(16)
    chain[0] = jnp.zeros((192, 128), F32)
    live = off_count[0]
    own.wait()

    partner = bulk + 1 - 2 * core

    def send_back(p, first, rows, target, send_sem, recv_sem, begin=0, end=16):
        def push_back(step, ty, tb, t):
            pltpu.make_async_remote_copy(
                src_ref=back.at[p, t // 2, pl.ds(first, rows)],
                dst_ref=target.at[me],
                send_sem=send_sem,
                recv_sem=recv_sem,
                device_id=(ty, tb),
                device_id_type=MESH,
            ).start()

        each_peer(sec, bulk, push_back, p, begin, end)
        if begin == 0:

            @pl.when(core != p)
            def _():
                push_back(0, sec, partner, sec * 32 + partner)

    def phase(p, carry):
        early = 4 * EARLY

        @pl.when(core == p)
        def _():
            part = got.at[p, pl.ds(0, early - 1)]
            pltpu.make_async_copy(part, part, go_recv.at[p, 0]).wait()

        @pl.when(core != p)
        def _():
            part = got.at[p, pl.ds(0, early)]
            pltpu.make_async_copy(part, part, go_recv.at[p, 0]).wait()

        @pl.when((p == 0) & (core == 1))
        def _():
            each_peer(sec, bulk, push)

        part = got.at[p, pl.ds(0, 64 - early)]
        pltpu.make_async_copy(part, part, go_recv.at[p, 1]).wait()

        def take(g, c2):
            h = g // 2
            q0 = pl.multiple_of(lax.rem(g, 2) * 16, 16)
            for tile in range(4):
                turned[tile * 128 : tile * 128 + 128, :] = dot_nn(
                    rows_of[...], side_by_side(got.at[p], 16 * g, tile)
                )

            def message_row(r):
                part = turned[r * 8 : r * 8 + 8, :]
                return jnp.concatenate([part[:, :128], part[:, 128:]], axis=0)

            rest = [message_row(60 + k) for k in range(4)]
            for c in range(4):
                v = vcls[c * 2 + h].astype(F32)
                picked = jnp.zeros((16, 128), F32)
                for k in range(4):
                    code = jnp.broadcast_to(rest[k][:, 8:9], (16, 128))
                    m = jnp.where(code == v, 1.0, 0.0)
                    mask[c * 4 + k] = m
                    picked = picked + m * rest[k]
                for i in range(6):
                    strain[(c * 2 + h) * 6 + i, pl.ds(q0, 16), :] = jnp.broadcast_to(
                        picked[:, i : i + 1], (16, 128)
                    )
            for a in range(4):
                for j in range(6):
                    sums = {}
                    for k in range(a, 4):
                        part = message_row(BASE[k] + a * 6 + j)
                        for c in range(a, 4):
                            term = mask[c * 4 + k] * part
                            sums[c] = sums[c] + term if c in sums else term
                    for c in range(a, 4):
                        i = static_row(c, h, a)
                        at = pl.multiple_of(j * 32 + q0, 16)
                        state[i, pl.ds(at, 16), :] = sums[c]
                        low[i, pl.ds(at, 16), :] = sums[c].astype(BF16)
            return c2

        lax.fori_loop(0, 4, take, 0)

        def row_scale(i, c2):
            r = ridx[i]
            ch = chrow[i] * 6
            z = diag_n[0, 0, r] * strain[ch]
            for k in range(1, 6):
                z = z + diag_n[k, 0, r] * strain[ch + k]
            rdiag[i] = 1.0 / (1.0 + 0.4 * jnp.tanh(z))
            return c2

        lax.fori_loop(0, ROWS, row_scale, 0, unroll=5)

        def contact_scale(c, c2):
            ch = cvol[c] * 6
            z = off_n[0, 0, c] * strain[ch]
            for k in range(1, 6):
                z = z + off_n[k, 0, c] * strain[ch + k]
            on = jnp.where(c < live, 1.0, 0.0).astype(F32)
            cscale[c] = (1.0 + 0.4 * jnp.tanh(z)) * on
            return c2

        lax.fori_loop(0, OFF, contact_scale, 0, unroll=8)

        def sweep(n, c2):
            def contact(c, c3):
                value = dot_nt(low[ccol[c]], off[c]).reshape(6, 32, 128)
                scaled = (value * cscale[c][None]).reshape(192, 128)
                chain[c + 1] = chain[prev[c]] + scaled
                return c3

            lax.fori_loop(0, OFF, contact, 0, unroll=16)

            def update(i, c3):
                r = ridx[i]
                own_part = dot_nt(low[i], diag[r]).reshape(6, 32, 128)
                extra = chain[last[i]].reshape(6, 32, 128)
                step = ((coupling[r] - extra) * rdiag[i][None] - own_part) * dinv[i][None]
                new = state[i] + step.reshape(192, 128)
                state[i] = new
                low[i] = new.astype(BF16)
                return c3

            lax.fori_loop(0, ROWS, update, 0, unroll=10)
            return c2

        lax.fori_loop(0, SWEEPS, sweep, 0)

        lane = iota((32, 128), 1)
        for h in range(2):
            last_rows = []
            for c in range(4):
                acc = jnp.zeros((192, 128), F32)
                for a in range(c + 1):
                    i = static_row(c, h, a)
                    x = state[i]
                    high = low[i]
                    acc = acc + dot_nt(high, weights[i])
                    acc = acc + dot_nt((x - high.astype(F32)).astype(BF16), weights[i])
                    for j in range(0, 6, 2):
                        at = (BASE[c] + a * 6 + j) * 8
                        for q in range(4):
                            cols = (q % 2) * 128
                            mixed[h * 2 + q // 2, at : at + 16, cols : cols + 128] = two_rows(
                                x[j * 32 + q * 8 : j * 32 + q * 8 + 8],
                                x[j * 32 + 32 + q * 8 : j * 32 + 40 + q * 8],
                            )
                t = acc[0:32]
                for j in range(1, 6):
                    t = t + pltpu.roll(acc[j * 32 : (j + 1) * 32], 8 * j, axis=1)
                t = t + pltpu.roll(t, 64, axis=1)
                v = vcls[c * 2 + h]
                tangent = aff[v] - t / (128.0 * (c + 1))
                last_rows.append(
                    jnp.where(lane < 48, tangent, jnp.where(lane == 64, v.astype(F32), 0.0))
                )
            for k in (0, 2):
                at = (60 + k) * 8
                for q in range(4):
                    cols = (q % 2) * 128
                    mixed[h * 2 + q // 2, at : at + 16, cols : cols + 128] = two_rows(
                        last_rows[k][q * 8 : q * 8 + 8], last_rows[k + 1][q * 8 : q * 8 + 8]
                    )

        write_messages(slots[...], mixed, back.at[p], 4)

        send_back(p, 48, 16, tails, tail_send, tail_recv)

        @pl.when(p == 0)
        def _():
            send_back(0, 0, 48, body, body_send, body_recv, 0, SPLIT)

        return carry

    lax.fori_loop(0, 2, phase, 0)
    send_back(0, 0, 48, body, body_send, body_recv, SPLIT, 16)
    mine_back = back.at[core, me // 2]
    own_tail = pltpu.make_async_copy(mine_back.at[pl.ds(48, 16)], tails.at[me], own_sems.at[0])
    own_body = pltpu.make_async_copy(mine_back.at[pl.ds(0, 48)], body.at[me], own_sems.at[1])
    own_tail.start()
    own_body.start()

    where_to = pmap[...]
    owner = where_to // ELEM
    volume = (lax.rem(where_to, ELEM) // 64).astype(F32)
    same_owner = iota((N_DEV, ELEM), 0) == owner
    own_tail.wait()
    landed = tails.at[pl.ds(0, N_DEV - 1)]
    pltpu.make_async_copy(landed, landed, tail_recv).wait()
    keep = pltpu.make_async_copy(tails, tail, own_sems.at[2])
    keep.start()
    turn = to_rows(16)[96:128]
    for g in range(8):
        out = dot_nn(turn, side_by_side(tails, 16 * g, 0))
        for c in range(4):
            for i in range(2):
                parts[c, 16 * g + 8 * i : 16 * g + 8 * i + 8, :] = out[
                    c * 8 : c * 8 + 8, i * 128 : (i + 1) * 128
                ]
    tangent = jnp.zeros((128, ELEM), F32)
    for c in range(4):
        part = parts[c]
        code = jnp.broadcast_to(part[:, 64:65], (N_DEV, ELEM))
        pick = jnp.where(same_owner & (code == volume), 1.0, 0.0).astype(BF16)
        tangent = tangent + dot_nn(jnp.transpose(part).astype(BF16), pick)
    weight = volume_ref[...]
    macro_rows = [srows[i : i + 1, :] for i in range(6)]
    residual = (
        assemble(grads, conn, apply_tangent(tangent, macro_rows, weight), small_e) - load_ref[...]
    )
    residual_ref[...] = residual
    mine[...] = jnp.broadcast_to(
        jnp.sum(jnp.sum(residual * residual, axis=1, keepdims=True), axis=0, keepdims=True),
        (1, 128),
    )
    norms[me] = mine[...]

    def push_norm(step, ty, tb, t):
        pltpu.make_async_remote_copy(
            src_ref=mine,
            dst_ref=norms.at[me],
            send_sem=norm_send,
            recv_sem=norm_recv,
            device_id=(ty, tb),
            device_id_type=MESH,
        ).start()

    each_peer(sec, bulk, push_norm)
    send_back(1, 0, 48, body, body_send, body_recv)
    trial = strain_rows(gather_nodes(residual, conn, small), grads)
    product_ref[...] = assemble(grads, conn, apply_tangent(tangent, trial, weight), small_e)
    arrived = norms.at[pl.ds(0, N_DEV - 1)]
    pltpu.make_async_copy(arrived, arrived, norm_recv).wait()
    total = jnp.sum(norms[...], axis=0)
    root = jnp.sqrt(total / (3.0 * 16384) + 1e-06)
    update_ref[...] = -jnp.minimum(1.0, 1.0 / root) * residual

    sent = send.at[pl.ds(0, N_DEV - 1)]
    pltpu.make_async_copy(sent, sent, go_send).wait()
    pltpu.make_async_copy(arrived, arrived, norm_send).wait()
    keep.wait()
    own_body.wait()
    pltpu.make_async_copy(landed, landed, tail_send).wait()
    rest = body.at[pl.ds(0, N_DEV - 1)]
    pltpu.make_async_copy(rest, rest, body_send).wait()
    pltpu.make_async_copy(rest, rest, body_recv).wait()


def unpack_kernel(
    residual, product, update, tail_hbm, body_hbm, pmap,
    out_residual, out_product, out_update, out_hbm,
    tail, body, parts, spread, rows, flat, result, load_sems, sems,
):
    loads = [
        pltpu.make_async_copy(tail_hbm, tail, load_sems.at[0]),
        pltpu.make_async_copy(body_hbm, body, load_sems.at[1]),
    ]
    for load in loads:
        load.start()
    out_residual[...] = residual[...]
    out_product[...] = product[...]
    out_update[...] = update[...]
    n = iota((1, LEVEL), 1)
    source = lax.rem(n, 6) * 128 + n // 6
    spread[...] = jnp.where(iota((LEVEL, LEVEL), 0) == source, 1.0, 0.0).astype(BF16)
    turn = to_rows(16)
    where_to = pmap[...].astype(F32)
    column = jnp.transpose(jnp.broadcast_to(where_to, (128, ELEM))).astype(I32)
    owner = column // ELEM
    volume = lax.rem(column, ELEM) // 64
    same_owner = iota((ELEM, N_DEV), 1) == owner
    for load in loads:
        load.wait()
    for tile in range(4):
        for g in range(8):
            source_ref, at = (body, tile) if tile < 3 else (tail, 0)
            got = dot_nn(turn, side_by_side(source_ref, 16 * g, at))
            for i in range(16):
                r = tile * 16 + i
                part = got[i * 8 : i * 8 + 8]
                if r < 60:
                    c = 0 if r < 6 else 1 if r < 18 else 2 if r < 36 else 3
                    a, j = (r - BASE[c]) // 6, r % 6
                    block = LEVEL0[a] + c - a
                    rows[
                        block * 128 + 16 * g : block * 128 + 16 * g + 16, j * 128 : (j + 1) * 128
                    ] = two_rows(part[:, :128], part[:, 128:])
                else:
                    for side in range(2):
                        parts[r - 60, 16 * g + 8 * side : 16 * g + 8 * side + 8, :] = part[
                            :, side * 128 : (side + 1) * 128
                        ]
    picks = []
    for c in range(4):
        code = jnp.transpose(parts[c])[64:65, :].astype(I32)
        picks.append(jnp.where(same_owner & (code == volume), 1.0, 0.0).astype(BF16))
    pick = jnp.concatenate(picks, axis=1)
    copies = []
    for a in range(4):
        at, end = LEVEL0[a] * 128, (LEVEL0[a] + 4 - a) * 128
        flat[at:end, :] = dot_nn(rows[at:end, :], spread[...]).astype(BF16)
        result[:, a * LEVEL : (a + 1) * LEVEL] = dot_nn(
            pick[:, a * 128 :], flat[at:end, :]
        ).astype(BF16)
        part = pl.ds(a * LEVEL, LEVEL)
        copy = pltpu.make_async_copy(result.at[:, part], out_hbm.at[:, part], sems.at[a])
        copy.start()
        copies.append(copy)
    for copy in copies:
        copy.wait()


def forces_of(grads_ref, s):
    g = [[grads_ref[3 * a + k : 3 * a + k + 1, :] for k in range(3)] for a in range(4)]
    out = []
    for a in range(4):
        gx, gy, gz = g[a]
        out.append(
            (
                gx * s[0] + gz * s[4] + gy * s[5],
                gy * s[1] + gz * s[3] + gx * s[5],
                gz * s[2] + gy * s[3] + gx * s[4],
            )
        )
    return out


def assemble(grads_ref, conn_ref, stress, scratch):
    forces = forces_of(grads_ref, stress)
    total = jnp.zeros((8, NODE), F32)
    for a in range(4):
        scratch[...] = jnp.zeros_like(scratch)
        for k in range(3):
            f = forces[a][k]
            high = f.astype(BF16).astype(F32)
            rest = f - high
            middle = rest.astype(BF16).astype(F32)
            scratch[k : k + 1, :] = high
            scratch[8 + k : 9 + k, :] = middle
            scratch[16 + k : 17 + k, :] = rest - middle
        part = dot_nt(scratch[...].astype(BF16), node_onehot(conn_ref, a))
        total = total + (part[0:8] + part[8:16] + part[16:24])
    return total[0:3]


def apply_tangent(tangent, strain, weight):
    acc = tangent[0:8] * strain[0]
    for j in range(1, 6):
        acc = acc + tangent[8 * j : 8 * j + 8] * strain[j]
    acc = acc * weight
    return [acc[i : i + 1, :] for i in range(6)]


VMEM = pl.BlockSpec(memory_space=pltpu.VMEM)
SMEM = pl.BlockSpec(memory_space=pltpu.SMEM)
ANY = pl.BlockSpec(memory_space=pl.ANY)
DMA = pltpu.SemaphoreType.DMA


def params(collective_id=None, limit=48):
    return pltpu.CompilerParams(
        collective_id=collective_id,
        has_side_effects=collective_id is not None,
        vmem_limit_bytes=limit * 2**20,
    )


def on_device(
    displacement, nodal_load, connectivity, shape_grads, elem_volume, point_map, vol_blocks,
    c_affine, coupling, diag_blocks, diag_normal, off_blocks, off_row, off_col, off_normal,
    off_count, fluct_state,
):
    pmap = point_map.reshape(1, ELEM)
    volume = elem_volume.reshape(1, ELEM)
    smem = lambda n: pltpu.SMEM((n,), I32)
    vmem = pltpu.VMEM
    nodal = jax.ShapeDtypeStruct((3, NODE), F32)
    tail, body, residual, product, update = pl.pallas_call(
        step_kernel,
        out_shape=(
            jax.ShapeDtypeStruct((N_DEV, 16, 128), BF16),
            jax.ShapeDtypeStruct((N_DEV, 48, 128), BF16),
            nodal, nodal, nodal,
        ),
        in_specs=[VMEM] * 6 + [SMEM, VMEM] + [SMEM] * 5 + [ANY] * 4,
        out_specs=(ANY, ANY, VMEM, VMEM, VMEM),
        scratch_shapes=[
            vmem((ELEM, 4 * LEVEL), BF16),
            vmem((4, N_DEV, 128), F32),
            vmem((8, 512, 256), BF16),
            vmem((128, 128), BF16),
            vmem((128, 128), BF16),
            vmem((512, 256), F32),
            vmem((N_DEV, MSG, 128), BF16),
            vmem((LEVEL, LEVEL), BF16),
            vmem((1280, LEVEL), BF16),
            vmem((128, ELEM), F32),
            vmem((32, 128), F32),
            vmem((32, ELEM), F32),
            vmem((2, 64, MSG, 128), BF16),
            vmem((2, 64, MSG, 128), BF16),
            vmem((ROWS, 6, 1, 128), F32),
            vmem((ROWS, 128, 128), BF16),
            vmem((OFF, 128, 128), BF16),
            vmem((ROWS, 192, 128), F32),
            vmem((ROWS, 192, 128), BF16),
            vmem((OFF + 1, 192, 128), F32),
            vmem((16, 16, 128), F32),
            vmem((48, 32, 128), F32),
            vmem((ROWS, 32, 128), F32),
            vmem((OFF, 32, 128), F32),
            vmem((ROWS, 1, 128), F32),
            vmem((ROWS, 128, 128), BF16),
            vmem((8, 1, 128), F32),
            vmem((N_DEV, 16, 128), BF16),
            vmem((4, N_DEV, 128), F32),
            vmem((1, 128), F32),
            vmem((N_DEV, 1, 128), F32),
            smem(8), smem(ROWS), smem(ROWS), smem(ROWS), smem(ROWS),
            smem(OFF), smem(OFF), smem(OFF), smem(OFF),
            DMA((4,)), DMA((3,)), DMA, DMA((2, 2)), DMA, DMA, DMA, DMA, DMA, DMA,
        ],
        compiler_params=params(1, 60),
        name="step",
    )(
        displacement, nodal_load, connectivity, shape_grads, volume, pmap, vol_blocks, c_affine,
        diag_normal.transpose(2, 1, 0), off_normal.transpose(2, 1, 0), off_row.T, off_col.T,
        off_count, coupling.transpose(0, 2, 1, 3), diag_blocks[:, 0], off_blocks[:, 0],
        fluct_state,
    )
    return pl.pallas_call(
        unpack_kernel,
        out_shape=(nodal, nodal, nodal, jax.ShapeDtypeStruct((ELEM, 4 * LEVEL), BF16)),
        in_specs=[VMEM, VMEM, VMEM, ANY, ANY, VMEM],
        out_specs=(VMEM, VMEM, VMEM, ANY),
        scratch_shapes=[
            vmem((N_DEV, 16, 128), BF16),
            vmem((N_DEV, 48, 128), BF16),
            vmem((4, N_DEV, 128), F32),
            vmem((LEVEL, LEVEL), BF16),
            vmem((1280, LEVEL), BF16),
            vmem((1280, LEVEL), BF16),
            vmem((ELEM, 4 * LEVEL), BF16),
            DMA((2,)),
            DMA((4,)),
        ],
        compiler_params=params(None, 60),
        name="unpack",
    )(residual, product, update, tail, body, pmap)


def solution(mesh):
    both = ("sec", "bulk")
    return jax.shard_map(
        on_device,
        mesh=mesh,
        in_specs=(
            P(None, both), P(None, both), P(None, both), P(None, both), P(both), P(both),
            P("bulk", None), P("bulk", None, None), P(None, "bulk", None, None),
            P(None, "bulk", None, None), P(None, "bulk", None), P(None, "bulk", None, None),
            P(None, "bulk"), P(None, "bulk"), P(None, "bulk", None), P("bulk"), P(both, None),
        ),
        out_specs=(P(None, both), P(None, both), P(None, both), P(both, None)),
        check_vma=False,
    )
```
